32 devices in a mesh: lat: 8 (over y, x, core), lon: 4 (over z).
Axes of the slice: x: 2, y: 2, z: 4, core: 2. Of those that a mesh axis runs over, the one named last changes fastest.
Arguments:
- fields: bfloat16 [4, 64, 256, 640], P(None, 'lat', 'lon'), may hold values from -6 to 6
- kernel: float32 [64, 9, 3, 256], P('lat'), may hold values from -0.125 to 0.125
- theta: float32 [3, 640], P(None, 'lon'), may hold values from -4 to 4
- row_start: int32 [64], P('lat'), may hold values from 0 to 59, as said below
- row_count: int32 [64], P('lat'), may hold values from 1 to 9
- norm_gain: float32 [640], replicated, may hold values from 0.1 to 1.9
- w_in: bfloat16 [640, 1280], replicated, may hold values from -0.25 to 0.25
- b_in: float32 [1280], replicated, may hold values from -3 to 3
- w_out: bfloat16 [1280, 640], replicated, may hold values from -0.15625 to 0.15625
Outputs:
- block_out: bfloat16 [4, 64, 256, 640], P(None, 'lat', 'lon')
The draws below stay inside these ranges and needn't reach their ends.
Inputs may be any that keep to these rules, and one draw needn't show every extreme that they name: Output row i draws on rows row_start[i] to row_start[i] + row_count[i] - 1, all inside the grid and within 4 rows of i.
All inputs are finite; a program needn't handle non-finite values.
Results may differ from the reference program's by a relative error of at most 0.0085.
Values may be sent and summed in bfloat16 or wider, within the bound.
A program may use at most 192 MiB of HBM per device.

```python
import jax
import jax.numpy as jnp
from jax import lax

C = 640
HID = 1280
KBASIS = 3
REACH = 4
SLOTS = 9
ENS = 4
LAT_DEV = 8
NLAT = 64
NLON = 256


def support_rows(key):
    position = jnp.arange(NLAT, dtype=jnp.int32)
    lowest = jnp.maximum(position - REACH, 0)
    highest = jnp.minimum(position + REACH + 1, NLAT)
    counts = jax.random.randint(jax.random.fold_in(key, 11), (NLAT,), 1, SLOTS + 1)
    offsets = jax.random.randint(jax.random.fold_in(key, 12), (NLAT,), 0, SLOTS)
    offsets = offsets % (SLOTS - counts + 1)
    starts = position - REACH + offsets
    polar = (position < LAT_DEV) | (position >= NLAT - LAT_DEV)
    starts = jnp.where(polar, lowest, starts)
    counts = jnp.where(polar, highest - lowest, counts)
    return (starts.astype(jnp.int32), counts.astype(jnp.int32))


def draw_row_start(key, part):
    return support_rows(key)[0]


def draw_row_count(key, part):
    return support_rows(key)[1]


def shard_levels(stream_key, dims, shards, smallest, top_value):
    def one(dim, blocks):
        steps = jax.random.uniform(jax.random.fold_in(jax.random.fold_in(stream_key, 6), dim), (blocks,), jnp.float32, smallest / len(shards), top_value / len(shards))
        return jnp.repeat(jnp.exp(steps), dims[dim] // blocks).reshape((-1,) + (1,) * (len(dims) - dim - 1))

    level = one(*shards[0])
    for cut in shards[1:]:
        level = level * one(*cut)
    return level


def centred(stream_key, dims, deviation, bound, split=(), kind=jnp.bfloat16):
    loudness = shard_levels(stream_key, dims, split, -0.22, 0.18) if split else 1.0
    entries = jax.random.normal(stream_key, dims, jnp.float32) * deviation * loudness
    return jnp.minimum(jnp.maximum(entries, -bound), bound).astype(kind)


def setup_inputs(seed: int = 0) -> dict:
    key_of = jax.random.split(jax.random.key(seed), 10)
    return {
        "fields": centred(key_of[0], (ENS, NLAT, NLON, C), 1.0, 6.0, ((1, 8), (2, 4))),
        "kernel": centred(key_of[1], (NLAT, SLOTS, KBASIS, NLON), (NLON * SLOTS) ** -0.5, 0.125, ((0, 8),), jnp.float32),
        "theta": centred(key_of[2], (KBASIS, C), 1.0, 4.0, ((1, 4),), jnp.float32),
        "row_start": draw_row_start(jax.random.fold_in(key_of[9], 71), 0),
        "row_count": draw_row_count(jax.random.fold_in(key_of[9], 71), 0),
        "norm_gain": jnp.clip(1.0 + 0.18 * jax.random.normal(key_of[5], (C,), jnp.float32), 0.1, 1.9),
        "w_in": centred(key_of[6], (C, HID), C ** -0.5, 0.25),
        "b_in": centred(key_of[7], (HID,), 0.5, 3.0, (), jnp.float32),
        "w_out": centred(key_of[8], (HID, C), HID ** -0.5, 0.15625),
    }


def conv_member(member, kernel_hat, theta, row_start, row_count):
    spectrum = jnp.fft.fft(member.astype(jnp.float32), axis=1)
    total = jnp.zeros(spectrum.shape, spectrum.dtype)
    for slot in range(SLOTS):
        mixed = jnp.einsum('ikf,kc->ifc', kernel_hat[:, slot], theta)
        source = jnp.clip(row_start + slot, 0, NLAT - 1).astype(jnp.int32)
        live = (slot < row_count)[:, None, None]
        total = total + jnp.where(live, mixed * spectrum[source], jnp.zeros_like(total))
    return jnp.real(jnp.fft.ifft(total, axis=1)).astype(jnp.bfloat16)

def mlp_member(pair, norm_gain, w_in, b_in, w_out):
    member, conv = pair
    values = conv.astype(jnp.float32)
    mean = lax.optimization_barrier(jnp.mean(values, axis=-1, keepdims=True))
    var = lax.optimization_barrier(jnp.mean((values - mean) ** 2, axis=-1, keepdims=True))
    normed = ((values - mean) * lax.rsqrt(var + 1e-05) * norm_gain).astype(jnp.bfloat16)
    hidden = jax.nn.gelu(jnp.einsum('alc,ch->alh', normed.astype(jnp.float32), w_in.astype(jnp.float32)) + b_in, approximate=False).astype(jnp.bfloat16)
    branch = jnp.einsum('alh,hc->alc', hidden.astype(jnp.float32), w_out.astype(jnp.float32))
    return (member.astype(jnp.float32) + branch).astype(jnp.bfloat16)

def reference(fields, kernel, theta, row_start, row_count, norm_gain, w_in, b_in, w_out):
    kernel_hat = jnp.fft.fft(kernel, axis=3)
    conv = lax.map(lambda member: conv_member(member, kernel_hat, theta, row_start, row_count), fields)
    return lax.map(lambda pair: mlp_member(pair, norm_gain, w_in, b_in, w_out), (fields, conv))
```

```python
import functools
import math

import jax
import jax.numpy as jnp
from jax import lax
from jax.experimental import pallas as pl
from jax.experimental.pallas import tpu as pltpu
from jax.sharding import PartitionSpec as P

REACH = 4
WINDOW = 2 * REACH + 1
LANES = 128
MESH = pl.DeviceIdType.MESH


def windowed(kernel, row_start, row_count, first):
    rows, slots = kernel.shape[:2]
    centre = first + jnp.arange(rows, dtype=jnp.int32)
    shift = row_start - (centre - REACH)
    place = jnp.arange(WINDOW, dtype=jnp.int32)[None, :] - shift[:, None]
    total = jnp.zeros((rows, WINDOW) + kernel.shape[2:], jnp.float32)
    for slot in range(slots):
        hit = (place == slot) & (slot < row_count[:, None])
        total = total + jnp.where(hit[:, :, None, None], kernel[:, slot][:, None], 0.0)
    return jnp.roll(total[..., ::-1], 1, axis=-1)


def gather_kernel(
    L, T, members, fields, theta, taps, wide_out, base_out, theta_out,
    wide, build, theta_buf, send_sem, recv_sem, halo_send, halo_recv, th_send, th_recv, local_sem, out_sem, build_sem,
):
    lat, lon = lax.axis_index("lat"), lax.axis_index("lon")
    up, down = lax.rem(lat + 1, T), lax.rem(lat + T - 1, T)
    rows, cols = fields.shape[1], fields.shape[2]
    circle = wide.shape[2]
    basis = taps.shape[1] // WINDOW

    barrier = pltpu.get_barrier_semaphore()
    for step in range(1, L):
        pl.semaphore_signal(barrier, inc=1, device_id={"lon": lax.rem(lon + step, L)}, device_id_type=MESH)
    for other in (up, down):
        pl.semaphore_signal(barrier, inc=1, device_id={"lat": other}, device_id_type=MESH)
    pl.semaphore_wait(barrier, L + 1)

    def slab(owner):
        return wide.at[:, pl.ds(REACH, rows), pl.ds(pl.multiple_of(owner * cols, cols), cols), :]

    sends = []
    for step in range(1, L):
        peer = lax.rem(lon + step, L)
        sends.append(pltpu.make_async_remote_copy(
            src_ref=fields.at[pl.ds(peer * members, members)], dst_ref=slab(lon),
            send_sem=send_sem.at[step], recv_sem=recv_sem.at[step],
            device_id={"lon": peer}, device_id_type=MESH))
        sends.append(pltpu.make_async_remote_copy(
            src_ref=theta, dst_ref=theta_buf.at[lon],
            send_sem=th_send.at[step], recv_sem=th_recv.at[step],
            device_id={"lon": peer}, device_id_type=MESH))
    for copy in sends:
        copy.start()
    mine = pltpu.make_async_copy(fields.at[pl.ds(lon * members, members)], slab(lon), local_sem.at[0])
    mine_theta = pltpu.make_async_copy(theta, theta_buf.at[lon], local_sem.at[1])
    mine.start()
    mine_theta.start()
    mine.wait()
    mine_theta.wait()

    def forward(step, owner):
        part = pl.ds(pl.multiple_of(owner * cols, cols), cols)
        low = pltpu.make_async_remote_copy(
            src_ref=wide.at[:, pl.ds(REACH, REACH), part, :],
            dst_ref=wide.at[:, pl.ds(REACH + rows, REACH), part, :],
            send_sem=halo_send.at[0, step], recv_sem=halo_recv.at[0, step],
            device_id={"lat": down}, device_id_type=MESH)
        high = pltpu.make_async_remote_copy(
            src_ref=wide.at[:, pl.ds(rows, REACH), part, :],
            dst_ref=wide.at[:, pl.ds(0, REACH), part, :],
            send_sem=halo_send.at[1, step], recv_sem=halo_recv.at[1, step],
            device_id={"lat": up}, device_id_type=MESH)
        low.start()
        high.start()
        return [low, high]

    halos = forward(0, lon)

    def build_row(i, carry):
        slot = lax.rem(i, 2)
        out = pltpu.make_async_copy(build.at[slot], base_out.at[i], build_sem.at[slot])

        @pl.when(i >= 2)
        def _():
            out.wait()

        for w in range(WINDOW):
            for k in range(basis):
                line = taps[i, pl.ds(w * basis + k, 1), :]
                block = pltpu.roll(jnp.broadcast_to(line, (LANES, circle)), 0, 1, stride=1, stride_axis=0)
                build[slot, pl.ds(k * LANES, LANES), pl.ds(w * circle, circle)] = block.astype(jnp.bfloat16)
        out.start()
        return carry

    lax.fori_loop(0, rows, build_row, 0)
    for slot in range(2):
        pltpu.make_async_copy(build.at[slot], base_out.at[slot], build_sem.at[slot]).wait()

    for step in range(1, L):
        owner = lax.rem(lon + L - step, L)
        sends[2 * (step - 1)].wait_recv()
        sends[2 * (step - 1) + 1].wait_recv()
        halos += forward(step, owner)
    theta_copy = pltpu.make_async_copy(theta_buf, theta_out, local_sem.at[1])
    theta_copy.start()
    for copy in halos:
        copy.wait_recv()
    whole = pltpu.make_async_copy(wide, wide_out, out_sem)
    whole.start()
    for copy in sends + halos:
        copy.wait_send()
    theta_copy.wait()
    whole.wait()


def gather(fields, theta, taps, L, T):
    ens, rows, cols, chans = fields.shape
    members, circle = ens // L, cols * L
    basis = taps.shape[1] // WINDOW
    span = rows + 2 * REACH
    any_space = pl.BlockSpec(memory_space=pl.ANY)
    vmem = pl.BlockSpec(memory_space=pltpu.VMEM)
    wide = (members, span, circle, chans)
    base = (rows, basis * LANES, WINDOW * circle)
    dma = pltpu.SemaphoreType.DMA
    return pl.pallas_call(
        functools.partial(gather_kernel, L, T, members),
        out_shape=(
            jax.ShapeDtypeStruct(wide, jnp.bfloat16),
            jax.ShapeDtypeStruct(base, jnp.bfloat16),
            jax.ShapeDtypeStruct((L,) + theta.shape, jnp.float32),
        ),
        in_specs=[any_space, vmem, vmem],
        out_specs=(any_space, any_space, any_space),
        scratch_shapes=[
            pltpu.VMEM(wide, jnp.bfloat16),
            pltpu.VMEM((2,) + base[1:], jnp.bfloat16),
            pltpu.VMEM((L,) + theta.shape, jnp.float32),
            dma((L,)), dma((L,)), dma((2, L)), dma((2, L)), dma((L,)), dma((L,)), dma((2,)), dma, dma((2,)),
        ],
        compiler_params=pltpu.CompilerParams(
            collective_id=0, has_side_effects=True, vmem_limit_bytes=40 * 2**20),
        name="gather",
    )(fields, theta, taps)


def conv_kernel(base, wide, theta, out):
    row = pl.program_id(1)
    circle, chans = wide.shape[2], wide.shape[3]
    lhs = base[0]
    for h in range(circle // LANES):
        cut = h * LANES
        pieces = []
        for w in range(WINDOW):
            pieces.append(wide[0, row + w, pl.ds(cut, circle - cut), :])
            if cut:
                pieces.append(wide[0, row + w, pl.ds(0, cut), :])
        rhs = jnp.concatenate(pieces, axis=0)
        prod = jnp.dot(lhs, rhs, preferred_element_type=jnp.float32)
        total = prod[:LANES] * theta[0:1, :]
        for k in range(1, theta.shape[0]):
            total = total + prod[k * LANES:(k + 1) * LANES] * theta[k:k + 1, :]
        out[0, 0, pl.ds(cut, LANES), :] = total.astype(jnp.bfloat16)


def convolve(base, wide, theta):
    rows = base.shape[0]
    members, span, circle, chans = wide.shape
    return pl.pallas_call(
        conv_kernel,
        grid=(members, rows),
        out_shape=jax.ShapeDtypeStruct((members, rows, circle, chans), jnp.bfloat16),
        in_specs=[
            pl.BlockSpec((1,) + base.shape[1:], lambda e, i: (i, 0, 0)),
            pl.BlockSpec((1, span, circle, chans), lambda e, i: (e, 0, 0, 0)),
            pl.BlockSpec(theta.shape, lambda e, i: (0, 0)),
        ],
        out_specs=pl.BlockSpec((1, 1, circle, chans), lambda e, i: (e, i, 0, 0)),
        compiler_params=pltpu.CompilerParams(vmem_limit_bytes=60 * 2**20),
        name="convolve",
    )(base, wide, theta)


def mlp_kernel(
    L, members, tile, conv, fields, gain, w_in, b_in, w_out, out,
    got, held, res, send_sem, recv_sem, local_sem, out_sem,
):
    lon = lax.axis_index("lon")
    rows, cols, chans = got.shape[1:]

    barrier = pltpu.get_barrier_semaphore()
    for step in range(1, L):
        pl.semaphore_signal(barrier, inc=1, device_id={"lon": lax.rem(lon + step, L)}, device_id_type=MESH)
    pl.semaphore_wait(barrier, L - 1)

    def part(owner):
        return conv.at[:, :, pl.ds(pl.multiple_of(owner * cols, cols), cols), :]

    sends = []
    for step in range(1, L):
        peer = lax.rem(lon + step, L)
        sends.append(pltpu.make_async_remote_copy(
            src_ref=part(peer), dst_ref=got.at[pl.ds(lon * members, members)],
            send_sem=send_sem.at[step], recv_sem=recv_sem.at[step],
            device_id={"lon": peer}, device_id_type=MESH))
    for copy in sends:
        copy.start()
    mine = pltpu.make_async_copy(part(lon), got.at[pl.ds(lon * members, members)], local_sem.at[0])
    bring = pltpu.make_async_copy(fields, held, local_sem.at[1])
    mine.start()
    bring.start()
    mine.wait()
    bring.wait()

    outs = []
    for step in range(L):
        owner = lax.rem(lon + L - step, L)
        if step:
            sends[step - 1].wait_recv()

        def points(t, carry):
            member = owner * members + t // (rows // tile)
            at = pl.ds(lax.rem(t, rows // tile) * tile, tile)
            values = got[member, at].reshape(tile * cols, chans).astype(jnp.float32)
            mean = jnp.mean(values, axis=-1, keepdims=True)
            diff = values - mean
            var = jnp.mean(diff * diff, axis=-1, keepdims=True)
            normed = (diff * lax.rsqrt(var + 1e-05) * gain[...]).astype(jnp.bfloat16)
            hidden = jnp.dot(normed, w_in[...], preferred_element_type=jnp.float32) + b_in[...]
            hidden = (0.5 * hidden * (1.0 + lax.erf(hidden * math.sqrt(0.5)))).astype(jnp.bfloat16)
            branch = jnp.dot(hidden, w_out[...], preferred_element_type=jnp.float32)
            start = held[member, at].reshape(tile * cols, chans).astype(jnp.float32)
            res[member, at] = (start + branch).astype(jnp.bfloat16).reshape(tile, cols, chans)
            return carry

        lax.fori_loop(0, members * (rows // tile), points, 0)
        here = pl.ds(owner * members, members)
        outs.append(pltpu.make_async_copy(res.at[here], out.at[here], out_sem.at[step]))
        outs[-1].start()
    for copy in sends:
        copy.wait_send()
    for copy in outs:
        copy.wait()


def mlp(conv, fields, gain, w_in, b_in, w_out, L):
    ens, rows, cols, chans = fields.shape
    members = ens // L
    tile = max(d for d in range(1, rows + 1) if rows % d == 0 and d * cols <= 256)
    any_space = pl.BlockSpec(memory_space=pl.ANY)
    vmem = pl.BlockSpec(memory_space=pltpu.VMEM)
    dma = pltpu.SemaphoreType.DMA
    return pl.pallas_call(
        functools.partial(mlp_kernel, L, members, tile),
        out_shape=jax.ShapeDtypeStruct(fields.shape, jnp.bfloat16),
        in_specs=[any_space, any_space, vmem, vmem, vmem, vmem],
        out_specs=any_space,
        scratch_shapes=[
            pltpu.VMEM(fields.shape, jnp.bfloat16),
            pltpu.VMEM(fields.shape, jnp.bfloat16),
            pltpu.VMEM(fields.shape, jnp.bfloat16),
            dma((L,)), dma((L,)), dma((2,)), dma((L,)),
        ],
        compiler_params=pltpu.CompilerParams(
            collective_id=1, has_side_effects=True, vmem_limit_bytes=48 * 2**20),
        name="mlp",
    )(conv, fields, gain[None, :], w_in, b_in[None, :], w_out)


def with_halo(value, sides, width):
    for axis, dim in sides:
        size, length = (lax.axis_size(axis), value.shape[dim])
        up = [(i, (i + 1) % size) for i in range(size - 1)]
        down = [(j, i) for i, j in up]
        last = lax.slice_in_dim(value, length - width, length, axis=dim)
        initial = lax.slice_in_dim(value, 0, width, axis=dim)
        before = lax.ppermute(last, axis, up)
        after = lax.ppermute(initial, axis, down)
        value = jnp.concatenate([before, value, after], axis=dim)
    return value


def circle_tables(length):
    bins = length // 2 + 1
    points = jnp.arange(length, dtype=jnp.int32)
    freqs = jnp.arange(bins, dtype=jnp.int32)
    phase = points[:, None] * freqs[None, :] % length
    angle = phase.astype(jnp.float32) * (2.0 * math.pi / length)
    cosine = jnp.cos(angle)
    sine = jnp.sin(angle)
    onward = jnp.concatenate([cosine, -sine], axis=1)
    weight = jnp.where((freqs == 0) | (freqs == length // 2), 1.0, 2.0).astype(jnp.float32)
    backward = (
        jnp.concatenate([(cosine * weight[None, :]).T, (-sine * weight[None, :]).T], axis=0)
        / length
    )
    return (onward, backward, bins)


def forward(field, onward, bins):
    upper = onward.astype(jnp.bfloat16)
    lower = (onward - upper.astype(jnp.float32)).astype(jnp.bfloat16)
    spectrum = jnp.einsum("ejlc,lg->ejgc", field, upper, preferred_element_type=jnp.float32)
    spectrum = spectrum + jnp.einsum(
        "ejlc,lg->ejgc", field, lower, preferred_element_type=jnp.float32
    )
    return (spectrum[:, :, :bins], spectrum[:, :, bins:])


def mix_basis(kern_part, theta):
    mixed = kern_part[:, :, 0, :, None] * theta[0][None, None, None, :]
    for basis in range(1, kern_part.shape[2]):
        mixed = mixed + kern_part[:, :, basis, :, None] * theta[basis][None, None, None, :]
    return mixed


def spectral_shards(fields, kernel, theta, row_start, row_count, norm_gain, w_in, b_in, w_out):
    local = lax.all_to_all(fields, "lon", split_axis=3, concat_axis=2, tiled=True)
    members, band, circle, chans = local.shape
    onward, backward, bins = circle_tables(circle)
    widened = with_halo(local, (("lat", 1),), REACH)
    spec_re, spec_im = forward(widened, onward, bins)
    kern_all = jnp.einsum("irkm,mg->irkg", kernel, onward, precision=lax.Precision.HIGHEST)
    mixed_re = mix_basis(kern_all[..., :bins], theta)
    mixed_im = mix_basis(kern_all[..., bins:], theta)
    first_row = lax.axis_index("lat") * band - REACH
    span_rows = band + 2 * REACH
    slot_ids = jnp.arange(WINDOW, dtype=jnp.int32)
    offsets = row_start - first_row
    live_slot = slot_ids[None, :] < row_count[:, None]
    total_re = jnp.zeros((members, band, bins, chans), jnp.float32)
    total_im = jnp.zeros((members, band, bins, chans), jnp.float32)
    for span in range(span_rows):
        select = (live_slot & (offsets[:, None] + slot_ids[None, :] == span)).astype(jnp.float32)
        coef_re = jnp.einsum("is,isfc->ifc", select, mixed_re, precision=lax.Precision.HIGHEST)
        coef_im = jnp.einsum("is,isfc->ifc", select, mixed_im, precision=lax.Precision.HIGHEST)
        row_re = spec_re[:, span][:, None]
        row_im = spec_im[:, span][:, None]
        total_re = total_re + coef_re * row_re - coef_im * row_im
        total_im = total_im + coef_re * row_im + coef_im * row_re
    joined = jnp.concatenate([total_re, total_im], axis=2)
    conv = jnp.einsum("eigc,gl->eilc", joined, backward, precision=lax.Precision.HIGHEST).astype(
        jnp.bfloat16
    )
    values = lax.all_to_all(conv, "lon", split_axis=2, concat_axis=3, tiled=True).astype(
        jnp.float32
    )
    mean = jnp.mean(values, axis=-1, keepdims=True)
    var = jnp.mean((values - mean) ** 2, axis=-1, keepdims=True)
    normed = ((values - mean) * lax.rsqrt(var + 1e-05) * norm_gain).astype(jnp.bfloat16)
    hidden = jax.nn.gelu(
        jnp.einsum("eblc,ch->eblh", normed, w_in, preferred_element_type=jnp.float32) + b_in,
        approximate=False,
    ).astype(jnp.bfloat16)
    branch = jnp.einsum("eblh,hc->eblc", hidden, w_out, preferred_element_type=jnp.float32)
    return (fields.astype(jnp.float32) + branch).astype(jnp.bfloat16)


def shards(L, T, fields, kernel, theta, row_start, row_count, norm_gain, w_in, b_in, w_out):
    if fields.shape[0] % L:
        return spectral_shards(
            fields, kernel, theta, row_start, row_count, norm_gain, w_in, b_in, w_out
        )
    rows = fields.shape[1]
    taps = windowed(kernel, row_start, row_count, lax.axis_index("lat") * rows)
    taps = taps.reshape(rows, -1, taps.shape[-1])
    wide, base, parts = gather(fields, theta, taps, L, T)
    full = jnp.transpose(parts, (1, 0, 2)).reshape(theta.shape[0], -1)
    conv = convolve(base, wide, full)
    return mlp(conv, fields, norm_gain, w_in, b_in, w_out, L)


def solution(mesh):
    placed = (
        P(None, "lat", "lon", None),
        P("lat", None, None, None),
        P(None, "lon"),
        P("lat"),
        P("lat"),
        P(),
        P(),
        P(),
        P(),
    )
    return jax.shard_map(
        functools.partial(shards, mesh.shape["lon"], mesh.shape["lat"]),
        mesh=mesh, in_specs=placed, out_specs=P(None, "lat", "lon", None), check_vma=False,
    )
```

```python
import functools
import math

import jax
import jax.numpy as jnp
from jax import lax
from jax.experimental import pallas as pl
from jax.experimental.pallas import tpu as pltpu
from jax.sharding import PartitionSpec as P

REACH = 4
WINDOW = 2 * REACH + 1
LANES = 128
MESH = pl.DeviceIdType.MESH


def windowed(kernel, row_start, row_count, first):
    rows, slots = kernel.shape[:2]
    centre = first + jnp.arange(rows, dtype=jnp.int32)
    shift = row_start - (centre - REACH)
    place = jnp.arange(WINDOW, dtype=jnp.int32)[None, :] - shift[:, None]
    total = jnp.zeros((rows, WINDOW) + kernel.shape[2:], jnp.float32)
    for slot in range(slots):
        hit = (place == slot) & (slot < row_count[:, None])
        total = total + jnp.where(hit[:, :, None, None], kernel[:, slot][:, None], 0.0)
    return jnp.roll(total[..., ::-1], 1, axis=-1)


def block_kernel(
    L, T, members, fields, theta, taps, gain, w_in, b_in, w_out, out,
    wide, base, theta_buf, staged, got, held, res,
    send_sem, recv_sem, halo_send, halo_recv, th_send, th_recv, local_sem, back_send, back_recv, own_sem, out_sem,
):
    lat, lon = lax.axis_index("lat"), lax.axis_index("lon")
    up, down = lax.rem(lat + 1, T), lax.rem(lat + T - 1, T)
    ens, rows, cols, chans = held.shape
    circle = wide.shape[2]
    basis = theta.shape[0]

    bring = pltpu.make_async_copy(fields, held, local_sem.at[2])
    bring.start()
    barrier = pltpu.get_barrier_semaphore()
    for step in range(1, L):
        pl.semaphore_signal(barrier, inc=1, device_id={"lon": lax.rem(lon + step, L)}, device_id_type=MESH)
    for other in (up, down):
        pl.semaphore_signal(barrier, inc=1, device_id={"lat": other}, device_id_type=MESH)
    pl.semaphore_wait(barrier, L + 1)

    def lons(owner):
        return pl.ds(pl.multiple_of(owner * cols, cols), cols)

    chunks = [(0, REACH)] + ([(REACH, rows - REACH)] if rows > REACH else [])
    sends = []
    for c, (low, size) in enumerate(chunks):
        row = []
        for step in range(1, L):
            peer = lax.rem(lon + step, L)
            row.append(pltpu.make_async_remote_copy(
                src_ref=fields.at[pl.ds(peer * members, members), pl.ds(low, size)],
                dst_ref=wide.at[:, pl.ds(REACH + low, size), lons(lon), :],
                send_sem=send_sem.at[c, step], recv_sem=recv_sem.at[c, step],
                device_id={"lon": peer}, device_id_type=MESH))
            row[-1].start()
        sends.append(row)
    shared = []
    for step in range(1, L):
        shared.append(pltpu.make_async_remote_copy(
            src_ref=theta, dst_ref=theta_buf.at[lon],
            send_sem=th_send.at[step], recv_sem=th_recv.at[step],
            device_id={"lon": lax.rem(lon + step, L)}, device_id_type=MESH))
        shared[-1].start()
    mine = pltpu.make_async_copy(
        fields.at[pl.ds(lon * members, members)], wide.at[:, pl.ds(REACH, rows), lons(lon), :], local_sem.at[0])
    mine_theta = pltpu.make_async_copy(theta, theta_buf.at[lon], local_sem.at[1])
    mine.start()
    mine_theta.start()
    mine.wait()
    mine_theta.wait()

    def forward(side, step, owner):
        source, target, other = ((REACH, REACH + rows, down), (rows, 0, up))[side]
        copy = pltpu.make_async_remote_copy(
            src_ref=wide.at[:, pl.ds(source, REACH), lons(owner), :],
            dst_ref=wide.at[:, pl.ds(target, REACH), lons(owner), :],
            send_sem=halo_send.at[side, step], recv_sem=halo_recv.at[side, step],
            device_id={"lat": other}, device_id_type=MESH)
        copy.start()
        return copy

    lower, upper = [forward(0, 0, lon)], [forward(1, 0, lon)]

    def build_row(i, carry):
        for w in range(WINDOW):
            for k in range(basis):
                line = taps[i, pl.ds(w * basis + k, 1), :]
                turned = pltpu.roll(jnp.broadcast_to(line, (LANES, circle)), 0, 1, stride=1, stride_axis=0)
                base[i, pl.ds(k * LANES, LANES), pl.ds(w * circle, circle)] = turned.astype(jnp.bfloat16)
        return carry

    lax.fori_loop(0, rows, build_row, 0)

    owners = [lax.rem(lon + L - step, L) for step in range(L)]
    for step in range(1, L):
        sends[0][step - 1].wait_recv()
        lower.append(forward(0, step, owners[step]))
    for copy in shared:
        copy.wait_recv()
    scale = theta_buf[0]
    for owner in range(1, L):
        scale = scale + theta_buf[owner]
    for step in range(1, L):
        for row in sends[1:]:
            row[step - 1].wait_recv()
        upper.append(forward(1, step, owners[step]))
    for copy in lower:
        copy.wait_recv()

    def back(slot, step, e):
        peer = lax.rem(lon + step, L)
        return pltpu.make_async_remote_copy(
            src_ref=staged.at[e, slot, lons(peer), :], dst_ref=got.at[slot, lon * members + e],
            send_sem=back_send.at[slot, step, e], recv_sem=back_recv.at[slot, step, e],
            device_id={"lon": peer}, device_id_type=MESH)

    def own(slot, e):
        return pltpu.make_async_copy(
            staged.at[e, slot, lons(lon), :], got.at[slot, lon * members + e], own_sem.at[slot, e])

    def send_row(slot):
        for e in range(members):
            for step in range(1, L):
                back(slot, step, e).start()
            own(slot, e).start()

    def conv_row(slot, carry):
        i = lax.rem(slot + REACH, rows)
        for e in range(members):
            for h in range(circle // LANES):
                cut = h * LANES
                pieces = []
                for w in range(WINDOW):
                    pieces.append(wide[e, i + w, pl.ds(cut, circle - cut), :])
                    if cut:
                        pieces.append(wide[e, i + w, pl.ds(0, cut), :])
                prod = jnp.dot(base[i], jnp.concatenate(pieces, axis=0), preferred_element_type=jnp.float32)
                total = prod[:LANES] * scale[0:1, :]
                for k in range(1, basis):
                    total = total + prod[k * LANES:(k + 1) * LANES] * scale[k:k + 1, :]
                staged[e, slot, pl.ds(cut, LANES), :] = total.astype(jnp.bfloat16)
                if e == 0 and h == 0:
                    @pl.when(slot > 0)
                    def _():
                        send_row(slot - 1)
        return carry

    first = max(rows - REACH, 0)
    lax.fori_loop(0, first, conv_row, 0)
    for copy in upper:
        copy.wait_recv()
    lax.fori_loop(first, rows, conv_row, 0)
    for row in sends:
        for copy in row:
            copy.wait_send()
    for copy in shared + lower + upper:
        copy.wait_send()
    bring.wait()

    def mlp_row(slot, carry):
        i = lax.rem(slot + REACH, rows)
        for e in range(members):
            for step in range(1, L):
                back(slot, step, e).wait_recv()
            own(slot, e).wait()
        values = got[slot].reshape(ens * cols, chans).astype(jnp.float32)
        mean = jnp.mean(values, axis=-1, keepdims=True)
        diff = values - mean
        var = jnp.mean(diff * diff, axis=-1, keepdims=True)
        normed = (diff * lax.rsqrt(var + 1e-05) * gain[...]).astype(jnp.bfloat16)
        hidden = jnp.dot(normed, w_in[...], preferred_element_type=jnp.float32) + b_in[...]
        hidden = (0.5 * hidden * (1.0 + lax.erf(hidden * math.sqrt(0.5)))).astype(jnp.bfloat16)

        @pl.when(slot == 0)
        def _():
            send_row(rows - 1)

        branch = jnp.dot(hidden, w_out[...], preferred_element_type=jnp.float32)
        start = held[:, i].reshape(ens * cols, chans).astype(jnp.float32)
        res[slot] = (start + branch).astype(jnp.bfloat16).reshape(ens, cols, chans)

        @pl.when(slot > 0)
        def _():
            before = slot - 1
            pltpu.make_async_copy(res.at[before], out.at[:, lax.rem(before + REACH, rows)], out_sem.at[before]).start()
        return carry

    lax.fori_loop(0, rows, mlp_row, 0)
    pltpu.make_async_copy(res.at[rows - 1], out.at[:, (rows - 1 + REACH) % rows], out_sem.at[rows - 1]).start()
    for slot in range(rows):
        for e in range(members):
            for step in range(1, L):
                back(slot, step, e).wait_send()
        pltpu.make_async_copy(res.at[slot], out.at[:, (slot + REACH) % rows], out_sem.at[slot]).wait()


def block(fields, theta, taps, gain, w_in, b_in, w_out, L, T):
    ens, rows, cols, chans = fields.shape
    members, circle = ens // L, cols * L
    basis = theta.shape[0]
    any_space = pl.BlockSpec(memory_space=pl.ANY)
    vmem = pl.BlockSpec(memory_space=pltpu.VMEM)
    dma = pltpu.SemaphoreType.DMA
    bf16 = jnp.bfloat16
    return pl.pallas_call(
        functools.partial(block_kernel, L, T, members),
        out_shape=jax.ShapeDtypeStruct(fields.shape, bf16),
        in_specs=[any_space] + [vmem] * 6,
        out_specs=any_space,
        scratch_shapes=[
            pltpu.VMEM((members, rows + 2 * REACH, circle, chans), bf16),
            pltpu.VMEM((rows, basis * LANES, WINDOW * circle), bf16),
            pltpu.VMEM((L,) + theta.shape, jnp.float32),
            pltpu.VMEM((members, rows, circle, chans), bf16),
            pltpu.VMEM((rows, ens, cols, chans), bf16),
            pltpu.VMEM(fields.shape, bf16),
            pltpu.VMEM((rows, ens, cols, chans), bf16),
            dma((2, L)), dma((2, L)), dma((2, L)), dma((2, L)), dma((L,)), dma((L,)), dma((3,)),
            dma((rows, L, members)), dma((rows, L, members)), dma((rows, members)), dma((rows,)),
        ],
        compiler_params=pltpu.CompilerParams(
            collective_id=0, has_side_effects=True, vmem_limit_bytes=60 * 2**20),
        name="block",
    )(fields, theta, taps, gain[None, :], w_in, b_in[None, :], w_out)


def with_halo(value, sides, width):
    for axis, dim in sides:
        size, length = (lax.axis_size(axis), value.shape[dim])
        up = [(i, (i + 1) % size) for i in range(size - 1)]
        down = [(j, i) for i, j in up]
        last = lax.slice_in_dim(value, length - width, length, axis=dim)
        initial = lax.slice_in_dim(value, 0, width, axis=dim)
        before = lax.ppermute(last, axis, up)
        after = lax.ppermute(initial, axis, down)
        value = jnp.concatenate([before, value, after], axis=dim)
    return value


def circle_tables(length):
    bins = length // 2 + 1
    points = jnp.arange(length, dtype=jnp.int32)
    freqs = jnp.arange(bins, dtype=jnp.int32)
    phase = points[:, None] * freqs[None, :] % length
    angle = phase.astype(jnp.float32) * (2.0 * math.pi / length)
    cosine = jnp.cos(angle)
    sine = jnp.sin(angle)
    onward = jnp.concatenate([cosine, -sine], axis=1)
    weight = jnp.where((freqs == 0) | (freqs == length // 2), 1.0, 2.0).astype(jnp.float32)
    backward = (
        jnp.concatenate([(cosine * weight[None, :]).T, (-sine * weight[None, :]).T], axis=0)
        / length
    )
    return (onward, backward, bins)


def forward(field, onward, bins):
    upper = onward.astype(jnp.bfloat16)
    lower = (onward - upper.astype(jnp.float32)).astype(jnp.bfloat16)
    spectrum = jnp.einsum("ejlc,lg->ejgc", field, upper, preferred_element_type=jnp.float32)
    spectrum = spectrum + jnp.einsum(
        "ejlc,lg->ejgc", field, lower, preferred_element_type=jnp.float32
    )
    return (spectrum[:, :, :bins], spectrum[:, :, bins:])


def mix_basis(kern_part, theta):
    mixed = kern_part[:, :, 0, :, None] * theta[0][None, None, None, :]
    for basis in range(1, kern_part.shape[2]):
        mixed = mixed + kern_part[:, :, basis, :, None] * theta[basis][None, None, None, :]
    return mixed


def spectral_shards(fields, kernel, theta, row_start, row_count, norm_gain, w_in, b_in, w_out):
    local = lax.all_to_all(fields, "lon", split_axis=3, concat_axis=2, tiled=True)
    members, band, circle, chans = local.shape
    onward, backward, bins = circle_tables(circle)
    widened = with_halo(local, (("lat", 1),), REACH)
    spec_re, spec_im = forward(widened, onward, bins)
    kern_all = jnp.einsum("irkm,mg->irkg", kernel, onward, precision=lax.Precision.HIGHEST)
    mixed_re = mix_basis(kern_all[..., :bins], theta)
    mixed_im = mix_basis(kern_all[..., bins:], theta)
    first_row = lax.axis_index("lat") * band - REACH
    span_rows = band + 2 * REACH
    slot_ids = jnp.arange(WINDOW, dtype=jnp.int32)
    offsets = row_start - first_row
    live_slot = slot_ids[None, :] < row_count[:, None]
    total_re = jnp.zeros((members, band, bins, chans), jnp.float32)
    total_im = jnp.zeros((members, band, bins, chans), jnp.float32)
    for span in range(span_rows):
        select = (live_slot & (offsets[:, None] + slot_ids[None, :] == span)).astype(jnp.float32)
        coef_re = jnp.einsum("is,isfc->ifc", select, mixed_re, precision=lax.Precision.HIGHEST)
        coef_im = jnp.einsum("is,isfc->ifc", select, mixed_im, precision=lax.Precision.HIGHEST)
        row_re = spec_re[:, span][:, None]
        row_im = spec_im[:, span][:, None]
        total_re = total_re + coef_re * row_re - coef_im * row_im
        total_im = total_im + coef_re * row_im + coef_im * row_re
    joined = jnp.concatenate([total_re, total_im], axis=2)
    conv = jnp.einsum("eigc,gl->eilc", joined, backward, precision=lax.Precision.HIGHEST).astype(
        jnp.bfloat16
    )
    values = lax.all_to_all(conv, "lon", split_axis=2, concat_axis=3, tiled=True).astype(
        jnp.float32
    )
    mean = jnp.mean(values, axis=-1, keepdims=True)
    var = jnp.mean((values - mean) ** 2, axis=-1, keepdims=True)
    normed = ((values - mean) * lax.rsqrt(var + 1e-05) * norm_gain).astype(jnp.bfloat16)
    hidden = jax.nn.gelu(
        jnp.einsum("eblc,ch->eblh", normed, w_in, preferred_element_type=jnp.float32) + b_in,
        approximate=False,
    ).astype(jnp.bfloat16)
    branch = jnp.einsum("eblh,hc->eblc", hidden, w_out, preferred_element_type=jnp.float32)
    return (fields.astype(jnp.float32) + branch).astype(jnp.bfloat16)


def shards(L, T, fields, kernel, theta, row_start, row_count, norm_gain, w_in, b_in, w_out):
    if fields.shape[0] % L:
        return spectral_shards(
            fields, kernel, theta, row_start, row_count, norm_gain, w_in, b_in, w_out
        )
    rows = fields.shape[1]
    taps = windowed(kernel, row_start, row_count, lax.axis_index("lat") * rows)
    taps = taps.reshape(rows, -1, taps.shape[-1])
    chans = theta.shape[1]
    spread = jnp.zeros((theta.shape[0], chans * L), jnp.float32)
    spread = lax.dynamic_update_slice(spread, theta, (0, lax.axis_index("lon") * chans))
    return block(fields, spread, taps, norm_gain, w_in, b_in, w_out, L, T)


def solution(mesh):
    placed = (
        P(None, "lat", "lon", None),
        P("lat", None, None, None),
        P(None, "lon"),
        P("lat"),
        P("lat"),
        P(),
        P(),
        P(),
        P(),
    )
    return jax.shard_map(
        functools.partial(shards, mesh.shape["lon"], mesh.shape["lat"]),
        mesh=mesh, in_specs=placed, out_specs=P(None, "lat", "lon", None), check_vma=False,
    )
```

```python
import functools
import math

import jax
import jax.numpy as jnp
from jax import lax
from jax.experimental import pallas as pl
from jax.experimental.pallas import tpu as pltpu
from jax.sharding import PartitionSpec as P

REACH = 4
WINDOW = 2 * REACH + 1
LANES = 128
MESH = pl.DeviceIdType.MESH


def block_kernel(
    L, T, members, fields, theta, kern, starts, counts, gain, w_in_hbm, b_in, w_out_hbm, out,
    wide, base, taps, w_in, w_out, theta_buf, staged, got, held, res,
    send_sem, recv_sem, halo_send, halo_recv, th_send, th_recv, local_sem, back_send, back_recv, own_sem, out_sem,
):
    lat, lon = lax.axis_index("lat"), lax.axis_index("lon")
    up, down = lax.rem(lat + 1, T), lax.rem(lat + T - 1, T)
    ens, rows, cols, chans = held.shape
    circle = wide.shape[2]
    slots, basis = kern.shape[1:3]

    bring = pltpu.make_async_copy(fields, held, local_sem.at[2])
    bring.start()
    weights = [
        pltpu.make_async_copy(w_in_hbm, w_in, local_sem.at[3]),
        pltpu.make_async_copy(w_out_hbm, w_out, local_sem.at[4]),
    ]
    for copy in weights:
        copy.start()
    barrier = pltpu.get_barrier_semaphore()
    for step in range(1, L):
        pl.semaphore_signal(barrier, inc=1, device_id={"lon": lax.rem(lon + step, L)}, device_id_type=MESH)
    for other in (up, down):
        pl.semaphore_signal(barrier, inc=1, device_id={"lat": other}, device_id_type=MESH)
    pl.semaphore_wait(barrier, L + 1)

    def lons(owner):
        return pl.ds(pl.multiple_of(owner * cols, cols), cols)

    chunks = [(0, REACH)] + ([(REACH, rows - REACH)] if rows > REACH else [])
    sends = []
    for c, (low, size) in enumerate(chunks):
        row = []
        for step in range(1, L):
            peer = lax.rem(lon + step, L)
            row.append(pltpu.make_async_remote_copy(
                src_ref=fields.at[pl.ds(peer * members, members), pl.ds(low, size)],
                dst_ref=wide.at[:, pl.ds(REACH + low, size), lons(lon), :],
                send_sem=send_sem.at[c, step], recv_sem=recv_sem.at[c, step],
                device_id={"lon": peer}, device_id_type=MESH))
            row[-1].start()
        sends.append(row)
    shared = []
    for step in range(1, L):
        shared.append(pltpu.make_async_remote_copy(
            src_ref=theta, dst_ref=theta_buf.at[lon],
            send_sem=th_send.at[step], recv_sem=th_recv.at[step],
            device_id={"lon": lax.rem(lon + step, L)}, device_id_type=MESH))
        shared[-1].start()
    mine = pltpu.make_async_copy(
        fields.at[pl.ds(lon * members, members)], wide.at[:, pl.ds(REACH, rows), lons(lon), :], local_sem.at[0])
    mine_theta = pltpu.make_async_copy(theta, theta_buf.at[lon], local_sem.at[1])
    mine.start()
    mine_theta.start()
    mine.wait()
    mine_theta.wait()

    def forward(side, step, owner):
        source, target, other = ((REACH, REACH + rows, down), (rows, 0, up))[side]
        copy = pltpu.make_async_remote_copy(
            src_ref=wide.at[:, pl.ds(source, REACH), lons(owner), :],
            dst_ref=wide.at[:, pl.ds(target, REACH), lons(owner), :],
            send_sem=halo_send.at[side, step], recv_sem=halo_recv.at[side, step],
            device_id={"lat": other}, device_id_type=MESH)
        copy.start()
        return copy

    lower, upper = [forward(0, 0, lon)], [forward(1, 0, lon)]

    place = lax.broadcasted_iota(jnp.int32, (circle, circle), 0) + lax.broadcasted_iota(
        jnp.int32, (circle, circle), 1)
    flip = jnp.where((place == 0) | (place == circle), 1.0, 0.0).astype(jnp.bfloat16)

    def build_row(i, carry):
        for s in range(slots):
            taps[pl.ds(s * basis, basis), :] = kern[i, s]
        taps[...] = jnp.dot(taps[...].astype(jnp.bfloat16), flip, preferred_element_type=jnp.float32)
        shift = starts[i] - (lat * rows + i - REACH)
        count = counts[i]
        for w in range(WINDOW):
            slot = w - shift
            live = jnp.where((slot >= 0) & (slot < count), 1.0, 0.0)
            slot = jnp.clip(slot, 0, slots - 1)
            for k in range(basis):
                line = taps[pl.ds(slot * basis + k, 1), :] * live
                turned = pltpu.roll(jnp.broadcast_to(line, (LANES, circle)), 0, 1, stride=1, stride_axis=0)
                base[i, pl.ds(k * LANES, LANES), pl.ds(w * circle, circle)] = turned.astype(jnp.bfloat16)
        return carry

    lax.fori_loop(0, rows, build_row, 0)

    owners = [lax.rem(lon + L - step, L) for step in range(L)]
    for step in range(1, L):
        sends[0][step - 1].wait_recv()
        lower.append(forward(0, step, owners[step]))
    for copy in shared:
        copy.wait_recv()
    scale = jnp.concatenate([theta_buf[owner] for owner in range(L)], axis=1)
    for step in range(1, L):
        for row in sends[1:]:
            row[step - 1].wait_recv()
        upper.append(forward(1, step, owners[step]))
    for copy in lower:
        copy.wait_recv()

    def back(slot, step, e):
        peer = lax.rem(lon + step, L)
        return pltpu.make_async_remote_copy(
            src_ref=staged.at[e, slot, lons(peer), :], dst_ref=got.at[slot, lon * members + e],
            send_sem=back_send.at[slot, step, e], recv_sem=back_recv.at[slot, step, e],
            device_id={"lon": peer}, device_id_type=MESH)

    def own(slot, e):
        return pltpu.make_async_copy(
            staged.at[e, slot, lons(lon), :], got.at[slot, lon * members + e], own_sem.at[slot, e])

    def send_row(slot):
        for e in range(members):
            for step in range(1, L):
                back(slot, step, e).start()
            own(slot, e).start()

    def conv_row(slot, carry):
        i = lax.rem(slot + REACH, rows)
        for e in range(members):
            for h in range(circle // LANES):
                cut = h * LANES
                pieces = []
                for w in range(WINDOW):
                    pieces.append(wide[e, i + w, pl.ds(cut, circle - cut), :])
                    if cut:
                        pieces.append(wide[e, i + w, pl.ds(0, cut), :])
                prod = jnp.dot(base[i], jnp.concatenate(pieces, axis=0), preferred_element_type=jnp.float32)
                total = prod[:LANES] * scale[0:1, :]
                for k in range(1, basis):
                    total = total + prod[k * LANES:(k + 1) * LANES] * scale[k:k + 1, :]
                staged[e, slot, pl.ds(cut, LANES), :] = total.astype(jnp.bfloat16)
                if e == 0 and h == 0:
                    @pl.when(slot > 0)
                    def _():
                        send_row(slot - 1)
        return carry

    first = max(rows - REACH, 0)
    lax.fori_loop(0, first, conv_row, 0)
    for copy in upper:
        copy.wait_recv()
    lax.fori_loop(first, rows, conv_row, 0)
    for row in sends:
        for copy in row:
            copy.wait_send()
    for copy in shared + lower + upper:
        copy.wait_send()
    bring.wait()
    for copy in weights:
        copy.wait()

    def mlp_row(slot, carry):
        i = lax.rem(slot + REACH, rows)
        for e in range(members):
            for step in range(1, L):
                back(slot, step, e).wait_recv()
            own(slot, e).wait()
        values = got[slot].reshape(ens * cols, chans).astype(jnp.float32)
        mean = jnp.mean(values, axis=-1, keepdims=True)
        diff = values - mean
        var = jnp.mean(diff * diff, axis=-1, keepdims=True)
        normed = (diff * lax.rsqrt(var + 1e-05) * gain[...][None, :]).astype(jnp.bfloat16)
        hidden = jnp.dot(normed, w_in[...], preferred_element_type=jnp.float32) + b_in[...][None, :]
        hidden = (0.5 * hidden * (1.0 + lax.erf(hidden * math.sqrt(0.5)))).astype(jnp.bfloat16)

        @pl.when(slot == 0)
        def _():
            send_row(rows - 1)

        branch = jnp.dot(hidden, w_out[...], preferred_element_type=jnp.float32)
        start = held[:, i].reshape(ens * cols, chans).astype(jnp.float32)
        res[slot] = (start + branch).astype(jnp.bfloat16).reshape(ens, cols, chans)

        @pl.when(slot > 0)
        def _():
            before = slot - 1
            pltpu.make_async_copy(res.at[before], out.at[:, lax.rem(before + REACH, rows)], out_sem.at[before]).start()
        return carry

    lax.fori_loop(0, rows, mlp_row, 0)
    pltpu.make_async_copy(res.at[rows - 1], out.at[:, (rows - 1 + REACH) % rows], out_sem.at[rows - 1]).start()
    for slot in range(rows):
        for e in range(members):
            for step in range(1, L):
                back(slot, step, e).wait_send()
        pltpu.make_async_copy(res.at[slot], out.at[:, (slot + REACH) % rows], out_sem.at[slot]).wait()


def block(fields, theta, kern, starts, counts, gain, w_in, b_in, w_out, L, T):
    ens, rows, cols, chans = fields.shape
    members, circle = ens // L, cols * L
    basis = theta.shape[0]
    any_space = pl.BlockSpec(memory_space=pl.ANY)
    vmem = pl.BlockSpec(memory_space=pltpu.VMEM)
    smem = pl.BlockSpec(memory_space=pltpu.SMEM)
    dma = pltpu.SemaphoreType.DMA
    bf16 = jnp.bfloat16
    return pl.pallas_call(
        functools.partial(block_kernel, L, T, members),
        out_shape=jax.ShapeDtypeStruct(fields.shape, bf16),
        in_specs=[any_space, vmem, vmem, smem, smem, vmem, any_space, vmem, any_space],
        out_specs=any_space,
        scratch_shapes=[
            pltpu.VMEM((members, rows + 2 * REACH, circle, chans), bf16),
            pltpu.VMEM((rows, basis * LANES, WINDOW * circle), bf16),
            pltpu.VMEM((kern.shape[1] * basis, circle), jnp.float32),
            pltpu.VMEM(w_in.shape, bf16),
            pltpu.VMEM(w_out.shape, bf16),
            pltpu.VMEM((L,) + theta.shape, jnp.float32),
            pltpu.VMEM((members, rows, circle, chans), bf16),
            pltpu.VMEM((rows, ens, cols, chans), bf16),
            pltpu.VMEM(fields.shape, bf16),
            pltpu.VMEM((rows, ens, cols, chans), bf16),
            dma((2, L)), dma((2, L)), dma((2, L)), dma((2, L)), dma((L,)), dma((L,)), dma((5,)),
            dma((rows, L, members)), dma((rows, L, members)), dma((rows, members)), dma((rows,)),
        ],
        compiler_params=pltpu.CompilerParams(
            collective_id=0, has_side_effects=True, vmem_limit_bytes=46 * 2**20),
        name="block",
    )(fields, theta, kern, starts, counts, gain, w_in, b_in, w_out)


def with_halo(value, sides, width):
    for axis, dim in sides:
        size, length = (lax.axis_size(axis), value.shape[dim])
        up = [(i, (i + 1) % size) for i in range(size - 1)]
        down = [(j, i) for i, j in up]
        last = lax.slice_in_dim(value, length - width, length, axis=dim)
        initial = lax.slice_in_dim(value, 0, width, axis=dim)
        before = lax.ppermute(last, axis, up)
        after = lax.ppermute(initial, axis, down)
        value = jnp.concatenate([before, value, after], axis=dim)
    return value


def circle_tables(length):
    bins = length // 2 + 1
    points = jnp.arange(length, dtype=jnp.int32)
    freqs = jnp.arange(bins, dtype=jnp.int32)
    phase = points[:, None] * freqs[None, :] % length
    angle = phase.astype(jnp.float32) * (2.0 * math.pi / length)
    cosine = jnp.cos(angle)
    sine = jnp.sin(angle)
    onward = jnp.concatenate([cosine, -sine], axis=1)
    weight = jnp.where((freqs == 0) | (freqs == length // 2), 1.0, 2.0).astype(jnp.float32)
    backward = (
        jnp.concatenate([(cosine * weight[None, :]).T, (-sine * weight[None, :]).T], axis=0)
        / length
    )
    return (onward, backward, bins)


def forward(field, onward, bins):
    upper = onward.astype(jnp.bfloat16)
    lower = (onward - upper.astype(jnp.float32)).astype(jnp.bfloat16)
    spectrum = jnp.einsum("ejlc,lg->ejgc", field, upper, preferred_element_type=jnp.float32)
    spectrum = spectrum + jnp.einsum(
        "ejlc,lg->ejgc", field, lower, preferred_element_type=jnp.float32
    )
    return (spectrum[:, :, :bins], spectrum[:, :, bins:])


def mix_basis(kern_part, theta):
    mixed = kern_part[:, :, 0, :, None] * theta[0][None, None, None, :]
    for basis in range(1, kern_part.shape[2]):
        mixed = mixed + kern_part[:, :, basis, :, None] * theta[basis][None, None, None, :]
    return mixed


def spectral_shards(fields, kernel, theta, row_start, row_count, norm_gain, w_in, b_in, w_out):
    local = lax.all_to_all(fields, "lon", split_axis=3, concat_axis=2, tiled=True)
    members, band, circle, chans = local.shape
    onward, backward, bins = circle_tables(circle)
    widened = with_halo(local, (("lat", 1),), REACH)
    spec_re, spec_im = forward(widened, onward, bins)
    kern_all = jnp.einsum("irkm,mg->irkg", kernel, onward, precision=lax.Precision.HIGHEST)
    mixed_re = mix_basis(kern_all[..., :bins], theta)
    mixed_im = mix_basis(kern_all[..., bins:], theta)
    first_row = lax.axis_index("lat") * band - REACH
    span_rows = band + 2 * REACH
    slot_ids = jnp.arange(WINDOW, dtype=jnp.int32)
    offsets = row_start - first_row
    live_slot = slot_ids[None, :] < row_count[:, None]
    total_re = jnp.zeros((members, band, bins, chans), jnp.float32)
    total_im = jnp.zeros((members, band, bins, chans), jnp.float32)
    for span in range(span_rows):
        select = (live_slot & (offsets[:, None] + slot_ids[None, :] == span)).astype(jnp.float32)
        coef_re = jnp.einsum("is,isfc->ifc", select, mixed_re, precision=lax.Precision.HIGHEST)
        coef_im = jnp.einsum("is,isfc->ifc", select, mixed_im, precision=lax.Precision.HIGHEST)
        row_re = spec_re[:, span][:, None]
        row_im = spec_im[:, span][:, None]
        total_re = total_re + coef_re * row_re - coef_im * row_im
        total_im = total_im + coef_re * row_im + coef_im * row_re
    joined = jnp.concatenate([total_re, total_im], axis=2)
    conv = jnp.einsum("eigc,gl->eilc", joined, backward, precision=lax.Precision.HIGHEST).astype(
        jnp.bfloat16
    )
    values = lax.all_to_all(conv, "lon", split_axis=2, concat_axis=3, tiled=True).astype(
        jnp.float32
    )
    mean = jnp.mean(values, axis=-1, keepdims=True)
    var = jnp.mean((values - mean) ** 2, axis=-1, keepdims=True)
    normed = ((values - mean) * lax.rsqrt(var + 1e-05) * norm_gain).astype(jnp.bfloat16)
    hidden = jax.nn.gelu(
        jnp.einsum("eblc,ch->eblh", normed, w_in, preferred_element_type=jnp.float32) + b_in,
        approximate=False,
    ).astype(jnp.bfloat16)
    branch = jnp.einsum("eblh,hc->eblc", hidden, w_out, preferred_element_type=jnp.float32)
    return (fields.astype(jnp.float32) + branch).astype(jnp.bfloat16)


def shards(L, T, fields, kernel, theta, row_start, row_count, norm_gain, w_in, b_in, w_out):
    if fields.shape[0] % L:
        return spectral_shards(
            fields, kernel, theta, row_start, row_count, norm_gain, w_in, b_in, w_out
        )
    return block(fields, theta, kernel, row_start, row_count, norm_gain, w_in, b_in, w_out, L, T)


def solution(mesh):
    placed = (
        P(None, "lat", "lon", None),
        P("lat", None, None, None),
        P(None, "lon"),
        P("lat"),
        P("lat"),
        P(),
        P(),
        P(),
        P(),
    )
    return jax.shard_map(
        functools.partial(shards, mesh.shape["lon"], mesh.shape["lat"]),
        mesh=mesh, in_specs=placed, out_specs=P(None, "lat", "lon", None), check_vma=False,
    )
```

```python
import functools
import math

import jax
import jax.numpy as jnp
from jax import lax
from jax.experimental import pallas as pl
from jax.experimental.pallas import tpu as pltpu
from jax.sharding import PartitionSpec as P

REACH = 4
WINDOW = 2 * REACH + 1
LANES = 128
MESH = pl.DeviceIdType.MESH


def block_kernel(
    L, T, members, fields, theta, kern_hbm, starts_hbm, counts_hbm, gain_hbm, w_in_hbm, b_in_hbm, w_out_hbm, out,
    wide, base, taps, kern, starts, counts, gain, w_in, b_in, w_out, theta_buf, staged, got, held, res,
    send_sem, recv_sem, halo_send, halo_recv, th_send, th_recv, local_sem, back_send, back_recv, own_sem, out_sem,
):
    lat, lon = lax.axis_index("lat"), lax.axis_index("lon")
    up, down = lax.rem(lat + 1, T), lax.rem(lat + T - 1, T)
    ens, rows, cols, chans = held.shape
    circle = wide.shape[2]
    slots, basis = kern.shape[:2]

    bring = pltpu.make_async_copy(fields, held, local_sem.at[2])
    bring.start()
    pairs = ((kern_hbm, kern), (starts_hbm, starts), (counts_hbm, counts), (gain_hbm, gain),
             (w_in_hbm, w_in), (b_in_hbm, b_in), (w_out_hbm, w_out))
    loads = [pltpu.make_async_copy(a, b, local_sem.at[3 + n]) for n, (a, b) in enumerate(pairs)]
    for copy in loads:
        copy.start()
    barrier = pltpu.get_barrier_semaphore()
    for step in range(1, L):
        pl.semaphore_signal(barrier, inc=1, device_id={"lon": lax.rem(lon + step, L)}, device_id_type=MESH)
    for other in (up, down):
        pl.semaphore_signal(barrier, inc=1, device_id={"lat": other}, device_id_type=MESH)
    pl.semaphore_wait(barrier, L + 1)

    def lons(owner):
        return pl.ds(pl.multiple_of(owner * cols, cols), cols)

    chunks = [(0, REACH)] + ([(REACH, rows - REACH)] if rows > REACH else [])
    sends = []
    for c, (low, size) in enumerate(chunks):
        row = []
        for step in range(1, L):
            peer = lax.rem(lon + step, L)
            row.append(pltpu.make_async_remote_copy(
                src_ref=fields.at[pl.ds(peer * members, members), pl.ds(low, size)],
                dst_ref=wide.at[:, pl.ds(REACH + low, size), lons(lon), :],
                send_sem=send_sem.at[c, step], recv_sem=recv_sem.at[c, step],
                device_id={"lon": peer}, device_id_type=MESH))
            row[-1].start()
        sends.append(row)
    shared = []
    for step in range(1, L):
        shared.append(pltpu.make_async_remote_copy(
            src_ref=theta, dst_ref=theta_buf.at[lon],
            send_sem=th_send.at[step], recv_sem=th_recv.at[step],
            device_id={"lon": lax.rem(lon + step, L)}, device_id_type=MESH))
        shared[-1].start()
    mine = pltpu.make_async_copy(
        fields.at[pl.ds(lon * members, members)], wide.at[:, pl.ds(REACH, rows), lons(lon), :], local_sem.at[0])
    mine_theta = pltpu.make_async_copy(theta, theta_buf.at[lon], local_sem.at[1])
    mine.start()
    mine_theta.start()
    mine.wait()
    mine_theta.wait()

    def forward(side, step, owner):
        source, target, other = ((REACH, REACH + rows, down), (rows, 0, up))[side]
        copy = pltpu.make_async_remote_copy(
            src_ref=wide.at[:, pl.ds(source, REACH), lons(owner), :],
            dst_ref=wide.at[:, pl.ds(target, REACH), lons(owner), :],
            send_sem=halo_send.at[side, step], recv_sem=halo_recv.at[side, step],
            device_id={"lat": other}, device_id_type=MESH)
        copy.start()
        return copy

    lower, upper = [forward(0, 0, lon)], [forward(1, 0, lon)]

    place = lax.broadcasted_iota(jnp.int32, (circle, circle), 0) + lax.broadcasted_iota(
        jnp.int32, (circle, circle), 1)
    flip = jnp.where((place == 0) | (place == circle), 1.0, 0.0).astype(jnp.bfloat16)

    for copy in loads[:3]:
        copy.wait()
    profiles = kern[...].reshape(slots * basis * rows, circle).astype(jnp.bfloat16)
    taps[...] = jnp.dot(profiles, flip, preferred_element_type=jnp.float32)

    def build_row(i, carry):
        shift = starts[i] - (lat * rows + i - REACH)
        count = counts[i]
        for w in range(WINDOW):
            slot = w - shift
            live = jnp.where((slot >= 0) & (slot < count), 1.0, 0.0)
            slot = jnp.clip(slot, 0, slots - 1)
            for k in range(basis):
                line = taps[pl.ds((slot * basis + k) * rows + i, 1), :] * live
                turned = pltpu.roll(jnp.broadcast_to(line, (LANES, circle)), 0, 1, stride=1, stride_axis=0)
                base[i, pl.ds(k * LANES, LANES), pl.ds(w * circle, circle)] = turned.astype(jnp.bfloat16)
        return carry

    lax.fori_loop(0, rows, build_row, 0)

    owners = [lax.rem(lon + L - step, L) for step in range(L)]
    for step in range(1, L):
        sends[0][step - 1].wait_recv()
        lower.append(forward(0, step, owners[step]))
    for copy in shared:
        copy.wait_recv()
    scale = jnp.concatenate([theta_buf[owner] for owner in range(L)], axis=1)
    for step in range(1, L):
        for row in sends[1:]:
            row[step - 1].wait_recv()
        upper.append(forward(1, step, owners[step]))
    for copy in lower:
        copy.wait_recv()

    def back(slot, step, e):
        peer = lax.rem(lon + step, L)
        return pltpu.make_async_remote_copy(
            src_ref=staged.at[e, slot, lons(peer), :], dst_ref=got.at[slot, lon * members + e],
            send_sem=back_send.at[slot, step, e], recv_sem=back_recv.at[slot, step, e],
            device_id={"lon": peer}, device_id_type=MESH)

    def own(slot, e):
        return pltpu.make_async_copy(
            staged.at[e, slot, lons(lon), :], got.at[slot, lon * members + e], own_sem.at[slot, e])

    def send_row(slot):
        for e in range(members):
            for step in range(1, L):
                back(slot, step, e).start()
            own(slot, e).start()

    def conv_row(slot, carry):
        i = lax.rem(slot + REACH, rows)
        for e in range(members):
            for h in range(circle // LANES):
                cut = h * LANES
                pieces = []
                for w in range(WINDOW):
                    pieces.append(wide[e, i + w, pl.ds(cut, circle - cut), :])
                    if cut:
                        pieces.append(wide[e, i + w, pl.ds(0, cut), :])
                prod = jnp.dot(base[i], jnp.concatenate(pieces, axis=0), preferred_element_type=jnp.float32)
                total = prod[:LANES] * scale[0:1, :]
                for k in range(1, basis):
                    total = total + prod[k * LANES:(k + 1) * LANES] * scale[k:k + 1, :]
                staged[e, slot, pl.ds(cut, LANES), :] = total.astype(jnp.bfloat16)
                if e == 0 and h == 0:
                    @pl.when(slot > 0)
                    def _():
                        send_row(slot - 1)
        return carry

    first = max(rows - REACH, 0)
    lax.fori_loop(0, first, conv_row, 0)
    for copy in upper:
        copy.wait_recv()
    lax.fori_loop(first, rows, conv_row, 0)
    for row in sends:
        for copy in row:
            copy.wait_send()
    for copy in shared + lower + upper:
        copy.wait_send()
    bring.wait()
    for copy in loads[3:]:
        copy.wait()

    def mlp_row(slot, carry):
        i = lax.rem(slot + REACH, rows)
        for e in range(members):
            for step in range(1, L):
                back(slot, step, e).wait_recv()
            own(slot, e).wait()
        values = got[slot].reshape(ens * cols, chans).astype(jnp.float32)
        mean = jnp.mean(values, axis=-1, keepdims=True)
        diff = values - mean
        var = jnp.mean(diff * diff, axis=-1, keepdims=True)
        normed = (diff * lax.rsqrt(var + 1e-05) * gain[...][None, :]).astype(jnp.bfloat16)
        hidden = jnp.dot(normed, w_in[...], preferred_element_type=jnp.float32) + b_in[...][None, :]
        hidden = (0.5 * hidden * (1.0 + lax.erf(hidden * math.sqrt(0.5)))).astype(jnp.bfloat16)

        @pl.when(slot == 0)
        def _():
            send_row(rows - 1)

        branch = jnp.dot(hidden, w_out[...], preferred_element_type=jnp.float32)
        start = held[:, i].reshape(ens * cols, chans).astype(jnp.float32)
        res[slot] = (start + branch).astype(jnp.bfloat16).reshape(ens, cols, chans)

        @pl.when(slot > 0)
        def _():
            before = slot - 1
            pltpu.make_async_copy(res.at[before], out.at[:, lax.rem(before + REACH, rows)], out_sem.at[before]).start()
        return carry

    lax.fori_loop(0, rows, mlp_row, 0)
    pltpu.make_async_copy(res.at[rows - 1], out.at[:, (rows - 1 + REACH) % rows], out_sem.at[rows - 1]).start()
    for slot in range(rows):
        for e in range(members):
            for step in range(1, L):
                back(slot, step, e).wait_send()
        pltpu.make_async_copy(res.at[slot], out.at[:, (slot + REACH) % rows], out_sem.at[slot]).wait()


def block(fields, theta, kern, starts, counts, gain, w_in, b_in, w_out, L, T):
    ens, rows, cols, chans = fields.shape
    members, circle = ens // L, cols * L
    basis = theta.shape[0]
    any_space = pl.BlockSpec(memory_space=pl.ANY)
    dma = pltpu.SemaphoreType.DMA
    bf16 = jnp.bfloat16
    return pl.pallas_call(
        functools.partial(block_kernel, L, T, members),
        out_shape=jax.ShapeDtypeStruct(fields.shape, bf16),
        in_specs=[pl.BlockSpec(memory_space=pltpu.HBM)] * 9,
        out_specs=any_space,
        scratch_shapes=[
            pltpu.VMEM((members, rows + 2 * REACH, circle, chans), bf16),
            pltpu.VMEM((rows, basis * LANES, WINDOW * circle), bf16),
            pltpu.VMEM((kern.shape[0] * basis * rows, circle), jnp.float32),
            pltpu.VMEM(kern.shape, jnp.float32),
            pltpu.SMEM(starts.shape, jnp.int32),
            pltpu.SMEM(counts.shape, jnp.int32),
            pltpu.VMEM(gain.shape, jnp.float32),
            pltpu.VMEM(w_in.shape, bf16),
            pltpu.VMEM(b_in.shape, jnp.float32),
            pltpu.VMEM(w_out.shape, bf16),
            pltpu.VMEM((L,) + theta.shape, jnp.float32),
            pltpu.VMEM((members, rows, circle, chans), bf16),
            pltpu.VMEM((rows, ens, cols, chans), bf16),
            pltpu.VMEM(fields.shape, bf16),
            pltpu.VMEM((rows, ens, cols, chans), bf16),
            dma((2, L)), dma((2, L)), dma((2, L)), dma((2, L)), dma((L,)), dma((L,)), dma((10,)),
            dma((rows, L, members)), dma((rows, L, members)), dma((rows, members)), dma((rows,)),
        ],
        compiler_params=pltpu.CompilerParams(
            collective_id=0, has_side_effects=True, vmem_limit_bytes=58 * 2**20),
        name="block",
    )(fields, theta, kern, starts, counts, gain, w_in, b_in, w_out)


def with_halo(value, sides, width):
    for axis, dim in sides:
        size, length = (lax.axis_size(axis), value.shape[dim])
        up = [(i, (i + 1) % size) for i in range(size - 1)]
        down = [(j, i) for i, j in up]
        last = lax.slice_in_dim(value, length - width, length, axis=dim)
        initial = lax.slice_in_dim(value, 0, width, axis=dim)
        before = lax.ppermute(last, axis, up)
        after = lax.ppermute(initial, axis, down)
        value = jnp.concatenate([before, value, after], axis=dim)
    return value


def circle_tables(length):
    bins = length // 2 + 1
    points = jnp.arange(length, dtype=jnp.int32)
    freqs = jnp.arange(bins, dtype=jnp.int32)
    phase = points[:, None] * freqs[None, :] % length
    angle = phase.astype(jnp.float32) * (2.0 * math.pi / length)
    cosine = jnp.cos(angle)
    sine = jnp.sin(angle)
    onward = jnp.concatenate([cosine, -sine], axis=1)
    weight = jnp.where((freqs == 0) | (freqs == length // 2), 1.0, 2.0).astype(jnp.float32)
    backward = (
        jnp.concatenate([(cosine * weight[None, :]).T, (-sine * weight[None, :]).T], axis=0)
        / length
    )
    return (onward, backward, bins)


def forward(field, onward, bins):
    upper = onward.astype(jnp.bfloat16)
    lower = (onward - upper.astype(jnp.float32)).astype(jnp.bfloat16)
    spectrum = jnp.einsum("ejlc,lg->ejgc", field, upper, preferred_element_type=jnp.float32)
    spectrum = spectrum + jnp.einsum(
        "ejlc,lg->ejgc", field, lower, preferred_element_type=jnp.float32
    )
    return (spectrum[:, :, :bins], spectrum[:, :, bins:])


def mix_basis(kern_part, theta):
    mixed = kern_part[:, :, 0, :, None] * theta[0][None, None, None, :]
    for basis in range(1, kern_part.shape[2]):
        mixed = mixed + kern_part[:, :, basis, :, None] * theta[basis][None, None, None, :]
    return mixed


def spectral_shards(fields, kernel, theta, row_start, row_count, norm_gain, w_in, b_in, w_out):
    local = lax.all_to_all(fields, "lon", split_axis=3, concat_axis=2, tiled=True)
    members, band, circle, chans = local.shape
    onward, backward, bins = circle_tables(circle)
    widened = with_halo(local, (("lat", 1),), REACH)
    spec_re, spec_im = forward(widened, onward, bins)
    kern_all = jnp.einsum("irkm,mg->irkg", kernel, onward, precision=lax.Precision.HIGHEST)
    mixed_re = mix_basis(kern_all[..., :bins], theta)
    mixed_im = mix_basis(kern_all[..., bins:], theta)
    first_row = lax.axis_index("lat") * band - REACH
    span_rows = band + 2 * REACH
    slot_ids = jnp.arange(WINDOW, dtype=jnp.int32)
    offsets = row_start - first_row
    live_slot = slot_ids[None, :] < row_count[:, None]
    total_re = jnp.zeros((members, band, bins, chans), jnp.float32)
    total_im = jnp.zeros((members, band, bins, chans), jnp.float32)
    for span in range(span_rows):
        select = (live_slot & (offsets[:, None] + slot_ids[None, :] == span)).astype(jnp.float32)
        coef_re = jnp.einsum("is,isfc->ifc", select, mixed_re, precision=lax.Precision.HIGHEST)
        coef_im = jnp.einsum("is,isfc->ifc", select, mixed_im, precision=lax.Precision.HIGHEST)
        row_re = spec_re[:, span][:, None]
        row_im = spec_im[:, span][:, None]
        total_re = total_re + coef_re * row_re - coef_im * row_im
        total_im = total_im + coef_re * row_im + coef_im * row_re
    joined = jnp.concatenate([total_re, total_im], axis=2)
    conv = jnp.einsum("eigc,gl->eilc", joined, backward, precision=lax.Precision.HIGHEST).astype(
        jnp.bfloat16
    )
    values = lax.all_to_all(conv, "lon", split_axis=2, concat_axis=3, tiled=True).astype(
        jnp.float32
    )
    mean = jnp.mean(values, axis=-1, keepdims=True)
    var = jnp.mean((values - mean) ** 2, axis=-1, keepdims=True)
    normed = ((values - mean) * lax.rsqrt(var + 1e-05) * norm_gain).astype(jnp.bfloat16)
    hidden = jax.nn.gelu(
        jnp.einsum("eblc,ch->eblh", normed, w_in, preferred_element_type=jnp.float32) + b_in,
        approximate=False,
    ).astype(jnp.bfloat16)
    branch = jnp.einsum("eblh,hc->eblc", hidden, w_out, preferred_element_type=jnp.float32)
    return (fields.astype(jnp.float32) + branch).astype(jnp.bfloat16)


def shards(L, T, fields, kernel, theta, row_start, row_count, norm_gain, w_in, b_in, w_out):
    if fields.shape[0] % L:
        return spectral_shards(
            fields, kernel, theta, row_start, row_count, norm_gain, w_in, b_in, w_out
        )
    kern = jnp.transpose(kernel, (1, 2, 0, 3))
    return block(fields, theta, kern, row_start, row_count, norm_gain, w_in, b_in, w_out, L, T)


def solution(mesh):
    placed = (
        P(None, "lat", "lon", None),
        P("lat", None, None, None),
        P(None, "lon"),
        P("lat"),
        P("lat"),
        P(),
        P(),
        P(),
        P(),
    )
    return jax.shard_map(
        functools.partial(shards, mesh.shape["lon"], mesh.shape["lat"]),
        mesh=mesh, in_specs=placed, out_specs=P(None, "lat", "lon", None), check_vma=False,
    )
```

```python
import functools
import math

import jax
import jax.numpy as jnp
from jax import lax
from jax.experimental import pallas as pl
from jax.experimental.pallas import tpu as pltpu
from jax.sharding import PartitionSpec as P

REACH = 4
WINDOW = 2 * REACH + 1
LANES = 128
MESH = pl.DeviceIdType.MESH


def block_kernel(
    L, T, members, fields, theta, kern_hbm, starts_hbm, counts_hbm, gain_hbm, w_in_hbm, b_in_hbm, w_out_hbm, out,
    wide, base, taps, kern, starts, counts, gain, w_in, b_in, w_out, theta_buf, staged, got, held, res,
    send_sem, recv_sem, halo_send, halo_recv, th_send, th_recv, local_sem, back_send, back_recv, own_sem, out_sem,
):
    lat, lon = lax.axis_index("lat"), lax.axis_index("lon")
    up, down = lax.rem(lat + 1, T), lax.rem(lat + T - 1, T)
    ens, rows, cols, chans = held.shape
    circle = wide.shape[2]
    slots, basis = kern.shape[:2]

    bring = pltpu.make_async_copy(fields, held, local_sem.at[2])
    bring.start()
    pairs = ((kern_hbm, kern), (starts_hbm, starts), (counts_hbm, counts), (gain_hbm, gain),
             (w_in_hbm, w_in), (b_in_hbm, b_in), (w_out_hbm, w_out))
    loads = [pltpu.make_async_copy(a, b, local_sem.at[3 + n]) for n, (a, b) in enumerate(pairs)]
    for copy in loads:
        copy.start()
    barrier = pltpu.get_barrier_semaphore()
    for step in range(1, L):
        pl.semaphore_signal(barrier, inc=1, device_id={"lon": lax.rem(lon + step, L)}, device_id_type=MESH)
    for other in (up, down):
        pl.semaphore_signal(barrier, inc=1, device_id={"lat": other}, device_id_type=MESH)
    pl.semaphore_wait(barrier, L + 1)

    def lons(owner):
        return pl.ds(pl.multiple_of(owner * cols, cols), cols)

    chunks = [(0, REACH)] + ([(REACH, rows - REACH)] if rows > REACH else [])
    split = (chans - 1) // LANES * LANES
    parts = [(0, split), (split, chans - split)] if split else [(0, chans)]
    sends = []
    for g, (first_chan, width) in enumerate(parts):
        sends.append([])
        for c, (low, size) in enumerate(chunks):
            row = []
            for step in range(1, L):
                peer = lax.rem(lon + step, L)
                row.append(pltpu.make_async_remote_copy(
                    src_ref=fields.at[
                        pl.ds(peer * members, members), pl.ds(low, size), :, pl.ds(first_chan, width)],
                    dst_ref=wide.at[:, pl.ds(REACH + low, size), lons(lon), pl.ds(first_chan, width)],
                    send_sem=send_sem.at[2 * g + c, step], recv_sem=recv_sem.at[2 * g + c, step],
                    device_id={"lon": peer}, device_id_type=MESH))
                row[-1].start()
            sends[-1].append(row)
    shared = []
    for step in range(1, L):
        shared.append(pltpu.make_async_remote_copy(
            src_ref=theta, dst_ref=theta_buf.at[lon],
            send_sem=th_send.at[step], recv_sem=th_recv.at[step],
            device_id={"lon": lax.rem(lon + step, L)}, device_id_type=MESH))
        shared[-1].start()
    mine = pltpu.make_async_copy(
        fields.at[pl.ds(lon * members, members)], wide.at[:, pl.ds(REACH, rows), lons(lon), :], local_sem.at[0])
    mine_theta = pltpu.make_async_copy(theta, theta_buf.at[lon], local_sem.at[1])
    mine.start()
    mine_theta.start()
    mine.wait()
    mine_theta.wait()

    def forward(side, g, step, owner):
        source, target, other = ((REACH, REACH + rows, down), (rows, 0, up))[side]
        chan = pl.ds(*parts[g])
        copy = pltpu.make_async_remote_copy(
            src_ref=wide.at[:, pl.ds(source, REACH), lons(owner), chan],
            dst_ref=wide.at[:, pl.ds(target, REACH), lons(owner), chan],
            send_sem=halo_send.at[2 * g + side, step], recv_sem=halo_recv.at[2 * g + side, step],
            device_id={"lat": other}, device_id_type=MESH)
        copy.start()
        return copy

    lower = [[forward(0, g, 0, lon)] for g in range(len(parts))]
    upper = [[forward(1, g, 0, lon)] for g in range(len(parts))]

    place = lax.broadcasted_iota(jnp.int32, (circle, circle), 0) + lax.broadcasted_iota(
        jnp.int32, (circle, circle), 1)
    flip = jnp.where((place == 0) | (place == circle), 1.0, 0.0).astype(jnp.bfloat16)

    for copy in loads[:3]:
        copy.wait()
    profiles = kern[...].reshape(slots * basis * rows, circle).astype(jnp.bfloat16)
    taps[...] = jnp.dot(profiles, flip, preferred_element_type=jnp.float32)

    def build_row(i, carry):
        shift = starts[i] - (lat * rows + i - REACH)
        count = counts[i]
        for w in range(WINDOW):
            slot = w - shift
            live = jnp.where((slot >= 0) & (slot < count), 1.0, 0.0)
            slot = jnp.clip(slot, 0, slots - 1)
            for k in range(basis):
                line = taps[pl.ds((slot * basis + k) * rows + i, 1), :] * live
                turned = pltpu.roll(jnp.broadcast_to(line, (LANES, circle)), 0, 1, stride=1, stride_axis=0)
                base[i, pl.ds(k * LANES, LANES), pl.ds(w * circle, circle)] = turned.astype(jnp.bfloat16)
        return carry

    lax.fori_loop(0, rows, build_row, 0)

    owners = [lax.rem(lon + L - step, L) for step in range(L)]

    def arrive(g):
        for step in range(1, L):
            sends[g][0][step - 1].wait_recv()
            lower[g].append(forward(0, g, step, owners[step]))
        for step in range(1, L):
            for row in sends[g][1:]:
                row[step - 1].wait_recv()
            upper[g].append(forward(1, g, step, owners[step]))
        for copy in lower[g]:
            copy.wait_recv()

    for copy in shared:
        copy.wait_recv()
    scale = jnp.concatenate([theta_buf[owner] for owner in range(L)], axis=1)

    def back(slot, step, e):
        peer = lax.rem(lon + step, L)
        return pltpu.make_async_remote_copy(
            src_ref=staged.at[e, slot, lons(peer), :], dst_ref=got.at[slot, lon * members + e],
            send_sem=back_send.at[slot, step, e], recv_sem=back_recv.at[slot, step, e],
            device_id={"lon": peer}, device_id_type=MESH)

    def own(slot, e):
        return pltpu.make_async_copy(
            staged.at[e, slot, lons(lon), :], got.at[slot, lon * members + e], own_sem.at[slot, e])

    def send_row(slot):
        for e in range(members):
            for step in range(1, L):
                back(slot, step, e).start()
            own(slot, e).start()

    def conv_row(first_chan, width, sending, slot, carry):
        chan = pl.ds(first_chan, width)
        i = lax.rem(slot + REACH, rows)
        for e in range(members):
            for h in range(circle // LANES):
                cut = h * LANES
                pieces = []
                for w in range(WINDOW):
                    pieces.append(wide[e, i + w, pl.ds(cut, circle - cut), chan])
                    if cut:
                        pieces.append(wide[e, i + w, pl.ds(0, cut), chan])
                prod = jnp.dot(base[i], jnp.concatenate(pieces, axis=0), preferred_element_type=jnp.float32)
                total = prod[:LANES] * scale[0:1, first_chan:first_chan + width]
                for k in range(1, basis):
                    total = total + prod[k * LANES:(k + 1) * LANES] * scale[k:k + 1, first_chan:first_chan + width]
                staged[e, slot, pl.ds(cut, LANES), chan] = total.astype(jnp.bfloat16)
                if sending and e == 0 and h == 0:
                    @pl.when(slot > 0)
                    def _():
                        send_row(slot - 1)
        return carry

    first = max(rows - REACH, 0)
    for g, part in enumerate(parts):
        arrive(g)
        lax.fori_loop(0, first, functools.partial(conv_row, *part, g == len(parts) - 1), 0)
    for copy in sum(upper, []):
        copy.wait_recv()
    lax.fori_loop(first, rows, functools.partial(conv_row, 0, chans, True), 0)
    for row in sum(sends, []):
        for copy in row:
            copy.wait_send()
    for copy in shared + sum(lower + upper, []):
        copy.wait_send()
    bring.wait()
    for copy in loads[3:]:
        copy.wait()

    def mlp_row(slot, carry):
        i = lax.rem(slot + REACH, rows)
        for e in range(members):
            for step in range(1, L):
                back(slot, step, e).wait_recv()
            own(slot, e).wait()
        values = got[slot].reshape(ens * cols, chans).astype(jnp.float32)
        mean = jnp.mean(values, axis=-1, keepdims=True)
        diff = values - mean
        var = jnp.mean(diff * diff, axis=-1, keepdims=True)
        normed = (diff * lax.rsqrt(var + 1e-05) * gain[...][None, :]).astype(jnp.bfloat16)
        hidden = jnp.dot(normed, w_in[...], preferred_element_type=jnp.float32) + b_in[...][None, :]
        hidden = (0.5 * hidden * (1.0 + lax.erf(hidden * math.sqrt(0.5)))).astype(jnp.bfloat16)

        @pl.when(slot == 0)
        def _():
            send_row(rows - 1)

        branch = jnp.dot(hidden, w_out[...], preferred_element_type=jnp.float32)
        start = held[:, i].reshape(ens * cols, chans).astype(jnp.float32)
        res[slot] = (start + branch).astype(jnp.bfloat16).reshape(ens, cols, chans)

        @pl.when(slot > 0)
        def _():
            before = slot - 1
            pltpu.make_async_copy(res.at[before], out.at[:, lax.rem(before + REACH, rows)], out_sem.at[before]).start()
        return carry

    lax.fori_loop(0, rows, mlp_row, 0)
    pltpu.make_async_copy(res.at[rows - 1], out.at[:, (rows - 1 + REACH) % rows], out_sem.at[rows - 1]).start()
    for slot in range(rows):
        for e in range(members):
            for step in range(1, L):
                back(slot, step, e).wait_send()
        pltpu.make_async_copy(res.at[slot], out.at[:, (slot + REACH) % rows], out_sem.at[slot]).wait()


def block(fields, theta, kern, starts, counts, gain, w_in, b_in, w_out, L, T):
    ens, rows, cols, chans = fields.shape
    members, circle = ens // L, cols * L
    basis = theta.shape[0]
    any_space = pl.BlockSpec(memory_space=pl.ANY)
    dma = pltpu.SemaphoreType.DMA
    bf16 = jnp.bfloat16
    return pl.pallas_call(
        functools.partial(block_kernel, L, T, members),
        out_shape=jax.ShapeDtypeStruct(fields.shape, bf16),
        in_specs=[pl.BlockSpec(memory_space=pltpu.HBM)] * 9,
        out_specs=any_space,
        scratch_shapes=[
            pltpu.VMEM((members, rows + 2 * REACH, circle, chans), bf16),
            pltpu.VMEM((rows, basis * LANES, WINDOW * circle), bf16),
            pltpu.VMEM((kern.shape[0] * basis * rows, circle), jnp.float32),
            pltpu.VMEM(kern.shape, jnp.float32),
            pltpu.SMEM(starts.shape, jnp.int32),
            pltpu.SMEM(counts.shape, jnp.int32),
            pltpu.VMEM(gain.shape, jnp.float32),
            pltpu.VMEM(w_in.shape, bf16),
            pltpu.VMEM(b_in.shape, jnp.float32),
            pltpu.VMEM(w_out.shape, bf16),
            pltpu.VMEM((L,) + theta.shape, jnp.float32),
            pltpu.VMEM((members, rows, circle, chans), bf16),
            pltpu.VMEM((rows, ens, cols, chans), bf16),
            pltpu.VMEM(fields.shape, bf16),
            pltpu.VMEM((rows, ens, cols, chans), bf16),
            dma((4, L)), dma((4, L)), dma((4, L)), dma((4, L)), dma((L,)), dma((L,)), dma((10,)),
            dma((rows, L, members)), dma((rows, L, members)), dma((rows, members)), dma((rows,)),
        ],
        compiler_params=pltpu.CompilerParams(
            collective_id=0, has_side_effects=True, vmem_limit_bytes=58 * 2**20),
        name="block",
    )(fields, theta, kern, starts, counts, gain, w_in, b_in, w_out)


def with_halo(value, sides, width):
    for axis, dim in sides:
        size, length = (lax.axis_size(axis), value.shape[dim])
        up = [(i, (i + 1) % size) for i in range(size - 1)]
        down = [(j, i) for i, j in up]
        last = lax.slice_in_dim(value, length - width, length, axis=dim)
        initial = lax.slice_in_dim(value, 0, width, axis=dim)
        before = lax.ppermute(last, axis, up)
        after = lax.ppermute(initial, axis, down)
        value = jnp.concatenate([before, value, after], axis=dim)
    return value


def circle_tables(length):
    bins = length // 2 + 1
    points = jnp.arange(length, dtype=jnp.int32)
    freqs = jnp.arange(bins, dtype=jnp.int32)
    phase = points[:, None] * freqs[None, :] % length
    angle = phase.astype(jnp.float32) * (2.0 * math.pi / length)
    cosine = jnp.cos(angle)
    sine = jnp.sin(angle)
    onward = jnp.concatenate([cosine, -sine], axis=1)
    weight = jnp.where((freqs == 0) | (freqs == length // 2), 1.0, 2.0).astype(jnp.float32)
    backward = (
        jnp.concatenate([(cosine * weight[None, :]).T, (-sine * weight[None, :]).T], axis=0)
        / length
    )
    return (onward, backward, bins)


def forward(field, onward, bins):
    upper = onward.astype(jnp.bfloat16)
    lower = (onward - upper.astype(jnp.float32)).astype(jnp.bfloat16)
    spectrum = jnp.einsum("ejlc,lg->ejgc", field, upper, preferred_element_type=jnp.float32)
    spectrum = spectrum + jnp.einsum(
        "ejlc,lg->ejgc", field, lower, preferred_element_type=jnp.float32
    )
    return (spectrum[:, :, :bins], spectrum[:, :, bins:])


def mix_basis(kern_part, theta):
    mixed = kern_part[:, :, 0, :, None] * theta[0][None, None, None, :]
    for basis in range(1, kern_part.shape[2]):
        mixed = mixed + kern_part[:, :, basis, :, None] * theta[basis][None, None, None, :]
    return mixed


def spectral_shards(fields, kernel, theta, row_start, row_count, norm_gain, w_in, b_in, w_out):
    local = lax.all_to_all(fields, "lon", split_axis=3, concat_axis=2, tiled=True)
    members, band, circle, chans = local.shape
    onward, backward, bins = circle_tables(circle)
    widened = with_halo(local, (("lat", 1),), REACH)
    spec_re, spec_im = forward(widened, onward, bins)
    kern_all = jnp.einsum("irkm,mg->irkg", kernel, onward, precision=lax.Precision.HIGHEST)
    mixed_re = mix_basis(kern_all[..., :bins], theta)
    mixed_im = mix_basis(kern_all[..., bins:], theta)
    first_row = lax.axis_index("lat") * band - REACH
    span_rows = band + 2 * REACH
    slot_ids = jnp.arange(WINDOW, dtype=jnp.int32)
    offsets = row_start - first_row
    live_slot = slot_ids[None, :] < row_count[:, None]
    total_re = jnp.zeros((members, band, bins, chans), jnp.float32)
    total_im = jnp.zeros((members, band, bins, chans), jnp.float32)
    for span in range(span_rows):
        select = (live_slot & (offsets[:, None] + slot_ids[None, :] == span)).astype(jnp.float32)
        coef_re = jnp.einsum("is,isfc->ifc", select, mixed_re, precision=lax.Precision.HIGHEST)
        coef_im = jnp.einsum("is,isfc->ifc", select, mixed_im, precision=lax.Precision.HIGHEST)
        row_re = spec_re[:, span][:, None]
        row_im = spec_im[:, span][:, None]
        total_re = total_re + coef_re * row_re - coef_im * row_im
        total_im = total_im + coef_re * row_im + coef_im * row_re
    joined = jnp.concatenate([total_re, total_im], axis=2)
    conv = jnp.einsum("eigc,gl->eilc", joined, backward, precision=lax.Precision.HIGHEST).astype(
        jnp.bfloat16
    )
    values = lax.all_to_all(conv, "lon", split_axis=2, concat_axis=3, tiled=True).astype(
        jnp.float32
    )
    mean = jnp.mean(values, axis=-1, keepdims=True)
    var = jnp.mean((values - mean) ** 2, axis=-1, keepdims=True)
    normed = ((values - mean) * lax.rsqrt(var + 1e-05) * norm_gain).astype(jnp.bfloat16)
    hidden = jax.nn.gelu(
        jnp.einsum("eblc,ch->eblh", normed, w_in, preferred_element_type=jnp.float32) + b_in,
        approximate=False,
    ).astype(jnp.bfloat16)
    branch = jnp.einsum("eblh,hc->eblc", hidden, w_out, preferred_element_type=jnp.float32)
    return (fields.astype(jnp.float32) + branch).astype(jnp.bfloat16)


def shards(L, T, fields, kernel, theta, row_start, row_count, norm_gain, w_in, b_in, w_out):
    if fields.shape[0] % L:
        return spectral_shards(
            fields, kernel, theta, row_start, row_count, norm_gain, w_in, b_in, w_out
        )
    kern = jnp.transpose(kernel, (1, 2, 0, 3))
    return block(fields, theta, kern, row_start, row_count, norm_gain, w_in, b_in, w_out, L, T)


def solution(mesh):
    placed = (
        P(None, "lat", "lon", None),
        P("lat", None, None, None),
        P(None, "lon"),
        P("lat"),
        P("lat"),
        P(),
        P(),
        P(),
        P(),
    )
    return jax.shard_map(
        functools.partial(shards, mesh.shape["lon"], mesh.shape["lat"]),
        mesh=mesh, in_specs=placed, out_specs=P(None, "lat", "lon", None), check_vma=False,
    )
```

```python
import functools
import math

import jax
import jax.numpy as jnp
from jax import lax
from jax.experimental import pallas as pl
from jax.experimental.pallas import tpu as pltpu
from jax.sharding import PartitionSpec as P

REACH = 4
WINDOW = 2 * REACH + 1
LANES = 128
MESH = pl.DeviceIdType.MESH


def block_kernel(
    L, T, members, fields, theta, kern_hbm, starts_hbm, counts_hbm, gain_hbm, w_in_hbm, b_in_hbm, w_out_hbm, out,
    wide, base, taps, kern, starts, counts, gain, w_in, b_in, w_out, theta_buf, staged, got, held, res,
    send_sem, recv_sem, halo_send, halo_recv, th_send, th_recv, local_sem, back_send, back_recv, own_sem, out_sem,
):
    lat, lon = lax.axis_index("lat"), lax.axis_index("lon")
    up, down = lax.rem(lat + 1, T), lax.rem(lat + T - 1, T)
    ens, rows, cols, chans = held.shape
    circle = wide.shape[2]
    slots, basis = kern.shape[:2]

    bring = pltpu.make_async_copy(fields, held, local_sem.at[2])
    bring.start()
    pairs = ((kern_hbm, kern), (starts_hbm, starts), (counts_hbm, counts), (gain_hbm, gain),
             (w_in_hbm, w_in), (b_in_hbm, b_in), (w_out_hbm, w_out))
    loads = [pltpu.make_async_copy(a, b, local_sem.at[3 + n]) for n, (a, b) in enumerate(pairs)]
    for copy in loads:
        copy.start()
    barrier = pltpu.get_barrier_semaphore()
    for step in range(1, L):
        pl.semaphore_signal(barrier, inc=1, device_id={"lon": lax.rem(lon + step, L)}, device_id_type=MESH)
    for other in (up, down):
        pl.semaphore_signal(barrier, inc=1, device_id={"lat": other}, device_id_type=MESH)
    pl.semaphore_wait(barrier, L + 1)

    def lons(owner):
        return pl.ds(pl.multiple_of(owner * cols, cols), cols)

    chunks = [(0, REACH)] + ([(REACH, rows - REACH)] if rows > REACH else [])
    sends = []
    for c, (low, size) in enumerate(chunks):
        row = []
        for step in range(1, L):
            peer = lax.rem(lon + step, L)
            row.append(pltpu.make_async_remote_copy(
                src_ref=fields.at[pl.ds(peer * members, members), pl.ds(low, size)],
                dst_ref=wide.at[:, pl.ds(REACH + low, size), lons(lon), :],
                send_sem=send_sem.at[c, step], recv_sem=recv_sem.at[c, step],
                device_id={"lon": peer}, device_id_type=MESH))
            row[-1].start()
        sends.append(row)
    shared = []
    for step in range(1, L):
        shared.append(pltpu.make_async_remote_copy(
            src_ref=theta, dst_ref=theta_buf.at[lon],
            send_sem=th_send.at[step], recv_sem=th_recv.at[step],
            device_id={"lon": lax.rem(lon + step, L)}, device_id_type=MESH))
        shared[-1].start()
    mine = pltpu.make_async_copy(
        fields.at[pl.ds(lon * members, members)], wide.at[:, pl.ds(REACH, rows), lons(lon), :], local_sem.at[0])
    mine_theta = pltpu.make_async_copy(theta, theta_buf.at[lon], local_sem.at[1])
    mine.start()
    mine_theta.start()
    mine.wait()
    mine_theta.wait()

    def forward(side, step, owner):
        source, target, other = ((REACH, REACH + rows, down), (rows, 0, up))[side]
        copy = pltpu.make_async_remote_copy(
            src_ref=wide.at[:, pl.ds(source, REACH), lons(owner), :],
            dst_ref=wide.at[:, pl.ds(target, REACH), lons(owner), :],
            send_sem=halo_send.at[side, step], recv_sem=halo_recv.at[side, step],
            device_id={"lat": other}, device_id_type=MESH)
        copy.start()
        return copy

    lower, upper = [forward(0, 0, lon)], [forward(1, 0, lon)]

    place = lax.broadcasted_iota(jnp.int32, (circle, circle), 0) + lax.broadcasted_iota(
        jnp.int32, (circle, circle), 1)
    flip = jnp.where((place == 0) | (place == circle), 1.0, 0.0).astype(jnp.bfloat16)

    for copy in loads[:3]:
        copy.wait()
    profiles = kern[...].reshape(slots * basis * rows, circle).astype(jnp.bfloat16)
    taps[...] = jnp.dot(profiles, flip, preferred_element_type=jnp.float32)

    def build_row(i, carry):
        shift = starts[i] - (lat * rows + i - REACH)
        count = counts[i]
        for w in range(WINDOW):
            slot = w - shift
            live = jnp.where((slot >= 0) & (slot < count), 1.0, 0.0)
            slot = jnp.clip(slot, 0, slots - 1)
            for k in range(basis):
                line = taps[pl.ds((slot * basis + k) * rows + i, 1), :] * live
                turned = pltpu.roll(jnp.broadcast_to(line, (LANES, circle)), 0, 1, stride=1, stride_axis=0)
                base[i, pl.ds(k * LANES, LANES), pl.ds(w * circle, circle)] = turned.astype(jnp.bfloat16)
        return carry

    lax.fori_loop(0, rows, build_row, 0)

    owners = [lax.rem(lon + L - step, L) for step in range(L)]
    for step in range(1, L):
        sends[0][step - 1].wait_recv()
        lower.append(forward(0, step, owners[step]))
    for copy in shared:
        copy.wait_recv()
    scale = jnp.concatenate([theta_buf[owner] for owner in range(L)], axis=1)
    for step in range(1, L):
        for row in sends[1:]:
            row[step - 1].wait_recv()
        upper.append(forward(1, step, owners[step]))
    for copy in lower:
        copy.wait_recv()

    def back(slot, step, e):
        peer = lax.rem(lon + step, L)
        return pltpu.make_async_remote_copy(
            src_ref=staged.at[e, slot, lons(peer), :], dst_ref=got.at[slot, lon * members + e],
            send_sem=back_send.at[slot, step, e], recv_sem=back_recv.at[slot, step, e],
            device_id={"lon": peer}, device_id_type=MESH)

    def own(slot, e):
        return pltpu.make_async_copy(
            staged.at[e, slot, lons(lon), :], got.at[slot, lon * members + e], own_sem.at[slot, e])

    blocks = circle // LANES

    def send_part(slot, h):
        for step in range(1, L):
            peer = lax.rem(lon + step, L)

            @pl.when((peer * cols + cols - 1) // LANES == h)
            def _():
                for e in range(members):
                    back(slot, step, e).start()

        if h == blocks - 1:
            for e in range(members):
                own(slot, e).start()

    def conv_row(slot, carry):
        i = lax.rem(slot + REACH, rows)
        for e in range(members):
            for h in range(circle // LANES):
                cut = h * LANES
                pieces = []
                for w in range(WINDOW):
                    pieces.append(wide[e, i + w, pl.ds(cut, circle - cut), :])
                    if cut:
                        pieces.append(wide[e, i + w, pl.ds(0, cut), :])
                prod = jnp.dot(base[i], jnp.concatenate(pieces, axis=0), preferred_element_type=jnp.float32)
                total = prod[:LANES] * scale[0:1, :]
                for k in range(1, basis):
                    total = total + prod[k * LANES:(k + 1) * LANES] * scale[k:k + 1, :]
                staged[e, slot, pl.ds(cut, LANES), :] = total.astype(jnp.bfloat16)
                if e == members - 1 and h > 0:
                    send_part(slot, h - 1)
                if e == 0 and h == 0:
                    @pl.when(slot > 0)
                    def _():
                        send_part(slot - 1, blocks - 1)
        return carry

    first = max(rows - REACH, 0)
    lax.fori_loop(0, first, conv_row, 0)
    for copy in upper:
        copy.wait_recv()
    lax.fori_loop(first, rows, conv_row, 0)
    for row in sends:
        for copy in row:
            copy.wait_send()
    for copy in shared + lower + upper:
        copy.wait_send()
    bring.wait()
    for copy in loads[3:]:
        copy.wait()

    def mlp_row(slot, carry):
        i = lax.rem(slot + REACH, rows)
        for e in range(members):
            for step in range(1, L):
                back(slot, step, e).wait_recv()
            own(slot, e).wait()
        values = got[slot].reshape(ens * cols, chans).astype(jnp.float32)
        mean = jnp.mean(values, axis=-1, keepdims=True)
        diff = values - mean
        var = jnp.mean(diff * diff, axis=-1, keepdims=True)
        normed = (diff * lax.rsqrt(var + 1e-05) * gain[...][None, :]).astype(jnp.bfloat16)
        hidden = jnp.dot(normed, w_in[...], preferred_element_type=jnp.float32) + b_in[...][None, :]
        hidden = (0.5 * hidden * (1.0 + lax.erf(hidden * math.sqrt(0.5)))).astype(jnp.bfloat16)

        @pl.when(slot == 0)
        def _():
            send_part(rows - 1, blocks - 1)

        branch = jnp.dot(hidden, w_out[...], preferred_element_type=jnp.float32)
        start = held[:, i].reshape(ens * cols, chans).astype(jnp.float32)
        res[slot] = (start + branch).astype(jnp.bfloat16).reshape(ens, cols, chans)

        @pl.when(slot > 0)
        def _():
            before = slot - 1
            pltpu.make_async_copy(res.at[before], out.at[:, lax.rem(before + REACH, rows)], out_sem.at[before]).start()
        return carry

    lax.fori_loop(0, rows, mlp_row, 0)
    pltpu.make_async_copy(res.at[rows - 1], out.at[:, (rows - 1 + REACH) % rows], out_sem.at[rows - 1]).start()
    for slot in range(rows):
        for e in range(members):
            for step in range(1, L):
                back(slot, step, e).wait_send()
        pltpu.make_async_copy(res.at[slot], out.at[:, (slot + REACH) % rows], out_sem.at[slot]).wait()


def block(fields, theta, kern, starts, counts, gain, w_in, b_in, w_out, L, T):
    ens, rows, cols, chans = fields.shape
    members, circle = ens // L, cols * L
    basis = theta.shape[0]
    any_space = pl.BlockSpec(memory_space=pl.ANY)
    dma = pltpu.SemaphoreType.DMA
    bf16 = jnp.bfloat16
    return pl.pallas_call(
        functools.partial(block_kernel, L, T, members),
        out_shape=jax.ShapeDtypeStruct(fields.shape, bf16),
        in_specs=[pl.BlockSpec(memory_space=pltpu.HBM)] * 9,
        out_specs=any_space,
        scratch_shapes=[
            pltpu.VMEM((members, rows + 2 * REACH, circle, chans), bf16),
            pltpu.VMEM((rows, basis * LANES, WINDOW * circle), bf16),
            pltpu.VMEM((kern.shape[0] * basis * rows, circle), jnp.float32),
            pltpu.VMEM(kern.shape, jnp.float32),
            pltpu.SMEM(starts.shape, jnp.int32),
            pltpu.SMEM(counts.shape, jnp.int32),
            pltpu.VMEM(gain.shape, jnp.float32),
            pltpu.VMEM(w_in.shape, bf16),
            pltpu.VMEM(b_in.shape, jnp.float32),
            pltpu.VMEM(w_out.shape, bf16),
            pltpu.VMEM((L,) + theta.shape, jnp.float32),
            pltpu.VMEM((members, rows, circle, chans), bf16),
            pltpu.VMEM((rows, ens, cols, chans), bf16),
            pltpu.VMEM(fields.shape, bf16),
            pltpu.VMEM((rows, ens, cols, chans), bf16),
            dma((2, L)), dma((2, L)), dma((2, L)), dma((2, L)), dma((L,)), dma((L,)), dma((10,)),
            dma((rows, L, members)), dma((rows, L, members)), dma((rows, members)), dma((rows,)),
        ],
        compiler_params=pltpu.CompilerParams(
            collective_id=0, has_side_effects=True, vmem_limit_bytes=58 * 2**20),
        name="block",
    )(fields, theta, kern, starts, counts, gain, w_in, b_in, w_out)


def with_halo(value, sides, width):
    for axis, dim in sides:
        size, length = (lax.axis_size(axis), value.shape[dim])
        up = [(i, (i + 1) % size) for i in range(size - 1)]
        down = [(j, i) for i, j in up]
        last = lax.slice_in_dim(value, length - width, length, axis=dim)
        initial = lax.slice_in_dim(value, 0, width, axis=dim)
        before = lax.ppermute(last, axis, up)
        after = lax.ppermute(initial, axis, down)
        value = jnp.concatenate([before, value, after], axis=dim)
    return value


def circle_tables(length):
    bins = length // 2 + 1
    points = jnp.arange(length, dtype=jnp.int32)
    freqs = jnp.arange(bins, dtype=jnp.int32)
    phase = points[:, None] * freqs[None, :] % length
    angle = phase.astype(jnp.float32) * (2.0 * math.pi / length)
    cosine = jnp.cos(angle)
    sine = jnp.sin(angle)
    onward = jnp.concatenate([cosine, -sine], axis=1)
    weight = jnp.where((freqs == 0) | (freqs == length // 2), 1.0, 2.0).astype(jnp.float32)
    backward = (
        jnp.concatenate([(cosine * weight[None, :]).T, (-sine * weight[None, :]).T], axis=0)
        / length
    )
    return (onward, backward, bins)


def forward(field, onward, bins):
    upper = onward.astype(jnp.bfloat16)
    lower = (onward - upper.astype(jnp.float32)).astype(jnp.bfloat16)
    spectrum = jnp.einsum("ejlc,lg->ejgc", field, upper, preferred_element_type=jnp.float32)
    spectrum = spectrum + jnp.einsum(
        "ejlc,lg->ejgc", field, lower, preferred_element_type=jnp.float32
    )
    return (spectrum[:, :, :bins], spectrum[:, :, bins:])


def mix_basis(kern_part, theta):
    mixed = kern_part[:, :, 0, :, None] * theta[0][None, None, None, :]
    for basis in range(1, kern_part.shape[2]):
        mixed = mixed + kern_part[:, :, basis, :, None] * theta[basis][None, None, None, :]
    return mixed


def spectral_shards(fields, kernel, theta, row_start, row_count, norm_gain, w_in, b_in, w_out):
    local = lax.all_to_all(fields, "lon", split_axis=3, concat_axis=2, tiled=True)
    members, band, circle, chans = local.shape
    onward, backward, bins = circle_tables(circle)
    widened = with_halo(local, (("lat", 1),), REACH)
    spec_re, spec_im = forward(widened, onward, bins)
    kern_all = jnp.einsum("irkm,mg->irkg", kernel, onward, precision=lax.Precision.HIGHEST)
    mixed_re = mix_basis(kern_all[..., :bins], theta)
    mixed_im = mix_basis(kern_all[..., bins:], theta)
    first_row = lax.axis_index("lat") * band - REACH
    span_rows = band + 2 * REACH
    slot_ids = jnp.arange(WINDOW, dtype=jnp.int32)
    offsets = row_start - first_row
    live_slot = slot_ids[None, :] < row_count[:, None]
    total_re = jnp.zeros((members, band, bins, chans), jnp.float32)
    total_im = jnp.zeros((members, band, bins, chans), jnp.float32)
    for span in range(span_rows):
        select = (live_slot & (offsets[:, None] + slot_ids[None, :] == span)).astype(jnp.float32)
        coef_re = jnp.einsum("is,isfc->ifc", select, mixed_re, precision=lax.Precision.HIGHEST)
        coef_im = jnp.einsum("is,isfc->ifc", select, mixed_im, precision=lax.Precision.HIGHEST)
        row_re = spec_re[:, span][:, None]
        row_im = spec_im[:, span][:, None]
        total_re = total_re + coef_re * row_re - coef_im * row_im
        total_im = total_im + coef_re * row_im + coef_im * row_re
    joined = jnp.concatenate([total_re, total_im], axis=2)
    conv = jnp.einsum("eigc,gl->eilc", joined, backward, precision=lax.Precision.HIGHEST).astype(
        jnp.bfloat16
    )
    values = lax.all_to_all(conv, "lon", split_axis=2, concat_axis=3, tiled=True).astype(
        jnp.float32
    )
    mean = jnp.mean(values, axis=-1, keepdims=True)
    var = jnp.mean((values - mean) ** 2, axis=-1, keepdims=True)
    normed = ((values - mean) * lax.rsqrt(var + 1e-05) * norm_gain).astype(jnp.bfloat16)
    hidden = jax.nn.gelu(
        jnp.einsum("eblc,ch->eblh", normed, w_in, preferred_element_type=jnp.float32) + b_in,
        approximate=False,
    ).astype(jnp.bfloat16)
    branch = jnp.einsum("eblh,hc->eblc", hidden, w_out, preferred_element_type=jnp.float32)
    return (fields.astype(jnp.float32) + branch).astype(jnp.bfloat16)


def shards(L, T, fields, kernel, theta, row_start, row_count, norm_gain, w_in, b_in, w_out):
    if fields.shape[0] % L:
        return spectral_shards(
            fields, kernel, theta, row_start, row_count, norm_gain, w_in, b_in, w_out
        )
    kern = jnp.transpose(kernel, (1, 2, 0, 3))
    return block(fields, theta, kern, row_start, row_count, norm_gain, w_in, b_in, w_out, L, T)


def solution(mesh):
    placed = (
        P(None, "lat", "lon", None),
        P("lat", None, None, None),
        P(None, "lon"),
        P("lat"),
        P("lat"),
        P(),
        P(),
        P(),
        P(),
    )
    return jax.shard_map(
        functools.partial(shards, mesh.shape["lon"], mesh.shape["lat"]),
        mesh=mesh, in_specs=placed, out_specs=P(None, "lat", "lon", None), check_vma=False,
    )
```
